32 devices in a mesh: wide: 8 (over z, x), narrow: 4 (over y, core).
Axes of the slice: x: 2, y: 2, z: 4, core: 2. Of those that a mesh axis runs over, the one named last changes fastest.
Arguments:
- star_pos: float32 [3, 2048], P(None, ('wide', 'narrow')), may hold values from -6 to 6
- star_vel: float32 [3, 2048], P(None, ('wide', 'narrow')), may hold values from -6 to 6
- star_mass: float32 [2048], P(('wide', 'narrow')), may hold values from 0.00048828125 to 0.0048828125
- star_acc: float32 [3, 2048], P(None, ('wide', 'narrow')), may hold values from -6 to 6
- star_jerk: float32 [3, 2048], P(None, ('wide', 'narrow')), may hold values from -120 to 120
- gal_pos: float32 [3, 16384], P(None, ('wide', 'narrow')), may hold values from -6 to 6
- gal_vel: float32 [3, 16384], P(None, ('wide', 'narrow')), may hold values from -6 to 6
- gal_mass: float32 [16384], P(('wide', 'narrow')), may hold values from 0.0009765625 to 0.009765625
- group_of: int32 [16384], P(('wide', 'narrow')), may hold values from 0 to 31, as said below
- let_send: int32 [32, 8, 1], P(('wide', 'narrow')), may hold values from -1 to 3, as said below
- star_leaf: int32 [128, 8], P(('wide', 'narrow')), may hold values from 0 to 7, as said below
Outputs:
- gal_vel_new: float32 [3, 16384], P(None, ('wide', 'narrow'))
- star_pos_new: float32 [3, 2048], P(None, ('wide', 'narrow'))
- star_vel_new: float32 [3, 2048], P(None, ('wide', 'narrow'))
The draws below stay inside these ranges and needn't reach their ends.
Inputs may be any that keep to these rules, and one draw needn't show every extreme that they name: `group_of`: within each leaf of 128 bodies every group number is held by exactly 4 bodies. `let_send`: entry [k, j, s] is a local leaf of device k sent to the device of wide index j with k's narrow index, or -1 for an empty slot; the leaves of one row are distinct; a device lists nothing for its own wide index; for some wide index j, every device whose wide index is not j lists a leaf for j, in every draw. `star_leaf`: the star blocks listed for one leaf are distinct.
All inputs are finite; a program needn't handle non-finite values.
Results may differ from the reference program's by a relative error of at most 0.0003.
Values sent between devices are 32-bit elements; how exact they have to be, the bound alone decides.
A program may use at most 64 MiB of HBM per device.

```python
import math
import jax
import jax.numpy as jnp
from jax import lax

LEAF = 128
GROUPS = 32
L_DEV = 4
S_DEV = 64
SLOTS = 1
KICK_BLOCKS = 8
NS = 2048
NLEAF = 128
NB = 16384
N_WIDE = 8
N_NARROW = 4
DEVICES = 32


def draw_group_of(key, part):
    keys = jax.random.split(key, NLEAF)
    base = jnp.arange(LEAF, dtype=jnp.int32) % GROUPS
    rows = jax.vmap(lambda row_key: jax.random.permutation(row_key, base))(keys)
    return rows.reshape(NB).astype(jnp.int32)


def draw_let_send(key, part):
    key_perm, key_busy, key_special, key_roll = jax.random.split(jax.random.fold_in(key, 11), 4)
    keys = jax.random.split(key_perm, DEVICES * N_WIDE)
    base = jnp.arange(L_DEV, dtype=jnp.int32)
    picks = jax.vmap(lambda row_key: jax.random.permutation(row_key, base)[:SLOTS])(keys)
    picks = picks.reshape(DEVICES, N_WIDE, SLOTS)
    busy = jax.random.randint(key_busy, (N_WIDE,), 1, 5)
    special = jax.random.randint(key_special, (), 0, N_WIDE)
    busy = jnp.where(jnp.arange(N_WIDE) == special, 4, busy)
    roll = jax.random.randint(key_roll, (DEVICES, N_WIDE, SLOTS), 0, 4)
    live = roll < busy[None, :, None]
    own = (jnp.arange(DEVICES) // N_NARROW)[:, None] == jnp.arange(N_WIDE)[None, :]
    live = jnp.logical_and(live, jnp.logical_not(own)[:, :, None])
    return jnp.where(live, picks, -1).astype(jnp.int32)


def draw_star_leaf(key, part):
    keys = jax.random.split(jax.random.fold_in(key, 23), NLEAF)
    base = jnp.arange(N_WIDE, dtype=jnp.int32)
    rows = jax.vmap(lambda row_key: jax.random.permutation(row_key, base)[:KICK_BLOCKS])(keys)
    return rows.astype(jnp.int32)


def shard_levels(stream_key, shape, cuts, least, top_value):
    level, own = 1.0, jax.random.fold_in(stream_key, 6)
    for position, blocks in cuts:
        steps = jnp.exp(jax.random.uniform(jax.random.fold_in(own, position), (blocks,), jnp.float32, least / len(cuts), top_value / len(cuts)))
        level = level * jnp.repeat(steps, shape[position] // blocks).reshape([-1 if axis == position else 1 for axis in range(len(shape))])
    return level


def bell_draw(rng, shape, width, bound, cuts=(), kind=jnp.bfloat16):
    loudness = shard_levels(rng, shape, cuts, -0.22, 0.18) if cuts else 1.0
    entries = jax.random.normal(rng, shape, jnp.float32) * width * loudness
    return jnp.minimum(jnp.maximum(entries, -bound), bound).astype(kind)


def setup_inputs(seed: int = 0) -> dict:
    streams_of = jax.random.split(jax.random.key(seed), 12)
    star_pos = bell_draw(streams_of[0], (3, NS), 1.0, 6.0, ((1, 32),), jnp.float32)
    star_vel = bell_draw(streams_of[1], (3, NS), 1.0, 6.0, ((1, 32),), jnp.float32)
    star_mass = jnp.clip(jnp.exp(math.log(0.0048828125) - 2.3025851 * jax.random.uniform(streams_of[2], (NS,), jnp.float32) ** shard_levels(streams_of[2], (NS,), ((0, 32),), -0.2, 0.2)), 0.00048828125, 0.0048828125)
    star_acc = bell_draw(streams_of[3], (3, NS), 1.0, 6.0, ((1, 32),), jnp.float32)
    star_jerk = bell_draw(streams_of[4], (3, NS), 20.0, 120.0, ((1, 32),), jnp.float32)
    gal_pos = bell_draw(streams_of[5], (3, NB), 1.0, 6.0, ((1, 32),), jnp.float32)
    gal_vel = bell_draw(streams_of[6], (3, NB), 1.0, 6.0, ((1, 32),), jnp.float32)
    gal_mass = jnp.clip(jnp.exp(math.log(0.009765625) - 2.3025851 * jax.random.uniform(streams_of[7], (NB,), jnp.float32) ** shard_levels(streams_of[7], (NB,), ((0, 32),), -0.2, 0.2)), 0.0009765625, 0.009765625)
    group_of = draw_group_of(jax.random.fold_in(streams_of[11], 71), 0)
    let_send = draw_let_send(jax.random.fold_in(streams_of[11], 71), 0)
    star_leaf = draw_star_leaf(jax.random.fold_in(streams_of[11], 71), 0)
    return {"star_pos": star_pos, "star_vel": star_vel, "star_mass": star_mass, "star_acc": star_acc, "star_jerk": star_jerk, "gal_pos": gal_pos, "gal_vel": gal_vel, "gal_mass": gal_mass, "group_of": group_of, "let_send": let_send, "star_leaf": star_leaf}


time_step = 0.25
soften_sq = 0.05

def by_blocks(kernel, arrays):
    total_rows = arrays[0].shape[1]
    block_rows = math.gcd(total_rows, 512)
    nblocks = total_rows // block_rows
    split = tuple((member.reshape(member.shape[0], nblocks, block_rows).transpose(1, 0, 2) for member in arrays))
    result = lax.map(kernel, split)
    return jax.tree.map(lambda piece: piece.transpose(1, 0, 2).reshape(piece.shape[1], total_rows), result)

def attract(tgt_pos, src_pos, src_mass):

    def kernel(pieces):
        here_pos = pieces[0]
        offset = src_pos[:, None, :] - here_pos[:, :, None]
        dist_sq = lax.optimization_barrier(jnp.sum(offset * offset, axis=0)) + soften_sq
        inverse = lax.rsqrt(dist_sq)
        weight = src_mass[None, :] * inverse * inverse * inverse
        return lax.optimization_barrier(jnp.sum(offset * weight[None], axis=2))
    return by_blocks(kernel, (tgt_pos,))

def hermite(tgt_pos, tgt_vel, src_pos, src_vel, src_mass):

    def kernel(pieces):
        here_pos, here_vel = pieces
        offset = src_pos[:, None, :] - here_pos[:, :, None]
        rel_vel = src_vel[:, None, :] - here_vel[:, :, None]
        dist_sq = lax.optimization_barrier(jnp.sum(offset * offset, axis=0)) + soften_sq
        inverse = lax.rsqrt(dist_sq)
        weight = src_mass[None, :] * inverse * inverse * inverse
        approach = 3.0 * lax.optimization_barrier(jnp.sum(offset * rel_vel, axis=0)) / dist_sq
        accel_sum = lax.optimization_barrier(jnp.sum(offset * weight[None], axis=2))
        jerk_sum = lax.optimization_barrier(jnp.sum((rel_vel - offset * approach[None]) * weight[None], axis=2))
        return (accel_sum, jerk_sum)
    return by_blocks(kernel, (tgt_pos, tgt_vel))

def reference(star_pos, star_vel, star_mass, star_acc, star_jerk, gal_pos, gal_vel, gal_mass, group_of, let_send, star_leaf):
    step_sq = time_step * time_step
    pred_pos = star_pos + time_step * star_vel + step_sq * 0.5 * star_acc + step_sq * time_step / 6.0 * star_jerk
    pred_vel = star_vel + time_step * star_acc + step_sq * 0.5 * star_jerk
    direct_acc, direct_jerk = hermite(pred_pos, pred_vel, pred_pos, pred_vel, star_mass)
    leaf_of = jnp.arange(NB, dtype=jnp.int32) // LEAF
    segment = leaf_of * GROUPS + group_of
    cell_mass = jax.ops.segment_sum(gal_mass, segment, num_segments=NLEAF * GROUPS)
    cell_mom = jax.vmap(lambda coord: jax.ops.segment_sum(coord * gal_mass, segment, num_segments=NLEAF * GROUPS))(gal_pos)
    cell_pos = cell_mom / cell_mass[None]
    local_size = L_DEV * LEAF
    group_range = jnp.arange(GROUPS, dtype=jnp.int32)
    star_range = jnp.arange(S_DEV, dtype=jnp.int32)

    def per_device(device):
        wide_idx = device // N_NARROW
        narrow_idx = device % N_NARROW
        sources = jnp.arange(N_WIDE, dtype=jnp.int32) * N_NARROW + narrow_idx
        slot_ids = let_send[sources, wide_idx]
        live = (slot_ids >= 0).astype(jnp.float32)
        leaf_idx = sources[:, None] * L_DEV + jnp.maximum(slot_ids, 0)
        cell_idx = (leaf_idx[:, :, None] * GROUPS + group_range[None, None, :]).reshape(-1)
        let_pos = cell_pos[:, cell_idx]
        let_mass = (cell_mass[cell_idx].reshape(N_WIDE, SLOTS, GROUPS) * live[:, :, None]).reshape(-1)
        own_cells = device * (L_DEV * GROUPS) + jnp.arange(L_DEV * GROUPS, dtype=jnp.int32)
        cells_pos = jnp.concatenate([cell_pos[:, own_cells], let_pos], axis=1)
        cells_mass = jnp.concatenate([cell_mass[own_cells], let_mass], axis=0)
        start = (device * local_size).astype(jnp.int32)
        bodies = lax.dynamic_slice_in_dim(gal_pos, start, local_size, 1)
        masses = lax.dynamic_slice_in_dim(gal_mass, start, local_size, 0)
        gal_acc = attract(bodies, bodies, masses) + attract(bodies, let_pos, let_mass)
        blocks = lax.dynamic_slice_in_dim(star_leaf, (device * L_DEV).astype(jnp.int32), L_DEV, 0)
        star_idx = (((blocks * N_NARROW + narrow_idx) * S_DEV)[:, :, None] + star_range[None, None, :]).reshape(L_DEV, KICK_BLOCKS * S_DEV)
        leaf_targets = bodies.reshape(3, L_DEV, LEAF)
        star_term = jax.vmap(lambda target, index: attract(target, pred_pos[:, index], star_mass[index]), in_axes=(1, 0), out_axes=1)(leaf_targets, star_idx)
        gal_acc = gal_acc + star_term.reshape(3, local_size)
        own_stars = lax.dynamic_slice_in_dim(pred_pos, (device * S_DEV).astype(jnp.int32), S_DEV, 1)
        star_cell = attract(own_stars, cells_pos, cells_mass)
        return (gal_acc, star_cell)
    gal_acc, cell_acc = lax.map(per_device, jnp.arange(DEVICES, dtype=jnp.int32))
    gal_acc = gal_acc.transpose(1, 0, 2).reshape(3, NB)
    cell_acc = cell_acc.transpose(1, 0, 2).reshape(3, NS)
    gal_vel_new = gal_vel + time_step * gal_acc
    new_acc = direct_acc + cell_acc
    star_vel_new = star_vel + time_step * 0.5 * (star_acc + new_acc) + step_sq / 12.0 * (star_jerk - direct_jerk)
    star_pos_new = star_pos + time_step * 0.5 * (star_vel + star_vel_new) + step_sq / 12.0 * (star_acc - new_acc)
    return (gal_vel_new, star_pos_new, star_vel_new)
```

```python
import functools

import jax
import jax.numpy as jnp
from jax import lax
from jax.experimental import pallas as pl
from jax.experimental.pallas import tpu as pltpu
from jax.sharding import PartitionSpec as P

GROUPS = 32
LANES = 128
ROWS = 8
MESH = pl.DeviceIdType.MESH

time_step = 0.25
soften_sq = 0.05


def loop(count, step, init, most=4):
    unroll = next(u for u in range(min(most, count), 0, -1) if count % u == 0)
    return lax.fori_loop(0, count, step, init, unroll=unroll)


def spread(row):
    return jnp.broadcast_to(row, (ROWS, row.shape[1]))


def column(block, index):
    return jnp.broadcast_to(block[:, index : index + 1], (ROWS, LANES))


def pull(source, mass, target, total):
    dx, dy, dz = (s - t for s, t in zip(source, target))
    inverse = lax.rsqrt(dx * dx + dy * dy + dz * dz + soften_sq)
    weight = mass * inverse * inverse * inverse
    return (total[0] + dx * weight, total[1] + dy * weight, total[2] + dz * weight)


def kernel(
    n_wide,
    n_narrow,
    star_pos,
    star_vel,
    star_mass,
    star_acc,
    star_jerk,
    gal_pos,
    gal_vel,
    gal_mass,
    group_of,
    let_send,
    star_leaf,
    gal_out,
    pos_out,
    vel_out,
    own,
    states,
    cell_out,
    cell_in,
    cols,
    srow,
    crow,
    prow,
    send_sem,
    recv_sem,
    cell_send_sem,
    cell_recv_sem,
):
    n_dev = n_wide * n_narrow
    wide, narrow = lax.axis_index("wide"), lax.axis_index("narrow")
    me = wide * n_narrow + narrow
    stars = star_pos.shape[1]
    bodies = gal_pos.shape[1]
    leaves, kicks = star_leaf.shape
    slots = LANES // GROUPS
    step_sq = time_step * time_step

    barrier = pltpu.get_barrier_semaphore()

    def greet(i, carry):
        peer = lax.rem(me + i, n_dev)
        pl.semaphore_signal(
            barrier,
            inc=1,
            device_id=(peer // n_narrow, lax.rem(peer, n_narrow)),
            device_id_type=MESH,
        )
        return carry

    lax.fori_loop(1, n_dev, greet, 0)

    lane = lax.broadcasted_iota(jnp.int32, (1, LANES), 1)
    lane4 = lax.broadcasted_iota(jnp.int32, (4, LANES), 1)
    lane8 = lax.broadcasted_iota(jnp.int32, (ROWS, LANES), 1)
    row8 = lax.broadcasted_iota(jnp.int32, (ROWS, LANES), 0)
    left = lane4 < stars

    spos, svel = star_pos[...], star_vel[...]
    sacc, sjerk = star_acc[...], star_jerk[...]
    pred_pos = (
        spos + time_step * svel + step_sq * 0.5 * sacc + step_sq * time_step / 6.0 * sjerk
    )
    pred_vel = svel + time_step * sacc + step_sq * 0.5 * sjerk
    pos4 = jnp.concatenate([pred_pos, star_mass[...]], axis=0)
    vel4 = jnp.concatenate([pred_vel, jnp.zeros((1, stars), jnp.float32)], axis=0)
    block = jnp.concatenate([pos4, vel4], axis=1)
    parity = lax.rem(wide + narrow, 2)
    block = jnp.where(parity == 0, block, pltpu.roll(block, stars, 1))
    own[0] = block
    states[me] = block
    both = jnp.concatenate([pos4, vel4], axis=0)
    targets = jnp.transpose(
        jnp.concatenate([both, jnp.zeros((ROWS, LANES - stars), jnp.float32)], axis=1)
    )

    gpos, gmass = gal_pos[...], gal_mass[...]
    body_lane = lax.broadcasted_iota(jnp.int32, (1, bodies), 1)
    segment = group_of[...] + (body_lane // (bodies // leaves)) * GROUPS
    onehot = (
        lax.broadcasted_iota(jnp.int32, (LANES, bodies), 0)
        == jnp.broadcast_to(segment, (LANES, bodies))
    ).astype(jnp.float32)
    moments = jnp.concatenate(
        [gpos * gmass, gmass, jnp.zeros((4, bodies), jnp.float32)], axis=0
    )
    sums = lax.dot_general(
        moments,
        onehot,
        (((1,), (1,)), ((), ())),
        precision=lax.Precision.HIGHEST,
        preferred_element_type=jnp.float32,
    )
    cells = jnp.where(row8 < 3, sums / spread(sums[3:4]), sums)
    crow[0] = cells

    group = lane // GROUPS
    part = jnp.bitwise_and(group - lax.rem(wide, slots), slots - 1)
    chosen = let_send[...]
    outgoing = jnp.zeros((n_wide, LANES), jnp.float32)
    pick = jnp.bitwise_and(group - chosen, slots - 1)
    for k in range(slots):
        turned = cells if k == 0 else pltpu.roll(cells, k * GROUPS, 1)
        base = jnp.zeros((1, LANES), jnp.float32)
        for c in range(4):
            base = jnp.where(part == c, turned[c : c + 1], base)
        outgoing = jnp.where(
            jnp.logical_and(pick == k, chosen >= 0),
            jnp.broadcast_to(base, (n_wide, LANES)),
            outgoing,
        )
    cell_out[:, 0, :] = outgoing
    cell_in[wide] = jnp.zeros((1, LANES), jnp.float32)

    pl.semaphore_wait(barrier, n_dev - 1)

    def state_copy(peer):
        return pltpu.make_async_remote_copy(
            src_ref=own.at[0],
            dst_ref=states.at[me],
            send_sem=send_sem,
            recv_sem=recv_sem,
            device_id=(peer // n_narrow, lax.rem(peer, n_narrow)),
            device_id_type=MESH,
        )

    def cell_copy(other):
        return pltpu.make_async_remote_copy(
            src_ref=cell_out.at[other],
            dst_ref=cell_in.at[wide],
            send_sem=cell_send_sem,
            recv_sem=cell_recv_sem,
            device_id=(other, narrow),
            device_id_type=MESH,
        )

    def send_state(i, carry):
        state_copy(lax.rem(me + i, n_dev)).start()
        return carry

    def send_cell(i, carry):
        cell_copy(lax.rem(wide + i, n_wide)).start()
        return carry

    lax.fori_loop(1, n_wide, send_cell, 0)
    lax.fori_loop(1, n_dev, send_state, 0)

    tiles = bodies // LANES
    body_rows = jnp.concatenate(
        [gpos, gmass, jnp.zeros((4, bodies), jnp.float32)], axis=0
    )
    for t in range(tiles):
        cols[t * LANES : (t + 1) * LANES, :] = jnp.transpose(
            body_rows[:, t * LANES : (t + 1) * LANES]
        )
    here = [
        [spread(gpos[c : c + 1, t * LANES : (t + 1) * LANES]) for c in range(3)]
        for t in range(tiles)
    ]

    def on_bodies(start, which, total):
        source = cols[pl.ds(pl.multiple_of(start, ROWS), ROWS), :]
        place = [column(source, c) for c in range(3)]
        mass = column(source, 3)
        return tuple(pull(place, mass, here[t], total[i]) for i, t in enumerate(which))

    every = tuple(range(tiles))
    zero = jnp.zeros((ROWS, LANES), jnp.float32)
    total = tuple((zero, zero, zero) for _ in every)
    total = loop(bodies // ROWS, lambda g, acc: on_bodies(g * ROWS, every, acc), total)

    pltpu.make_async_copy(
        states.at[pl.ds(0, n_dev - 1)], states.at[pl.ds(0, n_dev - 1)], recv_sem
    ).wait()
    pltpu.make_async_copy(
        cell_in.at[pl.ds(0, n_wide - 1)], cell_in.at[pl.ds(0, n_wide - 1)], cell_recv_sem
    ).wait()

    odd = n_narrow // 2

    def star_rows(i, carry):
        w = i // odd
        first = w * n_narrow + 2 * lax.rem(i, odd)
        flip = lax.rem(w, 2)
        even_block, odd_block = states[first + flip], states[first + 1 - flip]
        srow[i, 0:4, :] = jnp.where(left, even_block, odd_block)
        srow[i, 4:8, :] = pltpu.roll(jnp.where(left, odd_block, even_block), stars, 1)
        return carry

    pairs = n_dev // 2
    loop(pairs, star_rows, 0, 16)

    flip = lax.rem(narrow, 2)

    def star_cols(i, carry):
        even_block = states[(2 * i + flip) * n_narrow + narrow]
        odd_block = states[(2 * i + 1 - flip) * n_narrow + narrow]
        rows = jnp.where(left, even_block, odd_block)
        rows = jnp.concatenate([rows, jnp.zeros((4, LANES), jnp.float32)], axis=0)
        start = pl.multiple_of(bodies + i * LANES, LANES)
        cols[pl.ds(start, LANES), :] = jnp.transpose(rows)
        return carry

    loop(n_wide // 2, star_cols, 0)

    ess_start = bodies + n_wide * stars

    def ess_rows(e, carry):
        parts = []
        for c in range(4):
            row = jnp.zeros((1, LANES), jnp.float32)
            for k in range(slots):
                row = jnp.where(group == (c + k) % slots, cell_in[e * slots + k], row)
            parts.append(row if c == 0 else pltpu.roll(row, LANES - c * GROUPS, 1))
        parts.append(jnp.zeros((4, LANES), jnp.float32))
        rows = jnp.concatenate(parts, axis=0)
        crow[e + 1] = rows
        start = pl.multiple_of(ess_start + e * LANES, LANES)
        cols[pl.ds(start, LANES), :] = jnp.transpose(rows)
        return carry

    loop(n_wide // slots, ess_rows, 0)

    pieces = []
    for t in range(0, stars, ROWS):
        mine = targets[t : t + ROWS, :]
        place = [column(mine, c) for c in range(3)]
        speed = [column(mine, 4 + c) for c in range(3)]

        def hermite(i, acc):
            rows = [spread(srow[i, c : c + 1, :]) for c in range(7)]
            dx, dy, dz = (rows[c] - place[c] for c in range(3))
            ux, uy, uz = (rows[4 + c] - speed[c] for c in range(3))
            inverse = lax.rsqrt(dx * dx + dy * dy + dz * dz + soften_sq)
            square = inverse * inverse
            weight = rows[3] * inverse * square
            approach = 3.0 * (dx * ux + dy * uy + dz * uz) * square
            return (
                acc[0] + dx * weight,
                acc[1] + dy * weight,
                acc[2] + dz * weight,
                acc[3] + (ux - dx * approach) * weight,
                acc[4] + (uy - dy * approach) * weight,
                acc[5] + (uz - dz * approach) * weight,
            )

        acc = loop(pairs, hermite, (zero,) * 6)

        def cell_pull(i, part):
            rows = [spread(crow[i, c : c + 1, :]) for c in range(4)]
            return pull(rows[:3], rows[3], place, part)

        acc = loop(n_wide // slots + 1, cell_pull, acc[:3]) + acc[3:]
        piece = jnp.zeros((ROWS, LANES), jnp.float32)
        for c in range(6):
            piece = jnp.where(lane8 == c, jnp.sum(acc[c], axis=1, keepdims=True), piece)
        pieces.append(piece)
    result = jnp.transpose(jnp.concatenate(pieces, axis=0))
    new_acc, new_jerk = result[0:3], result[3:6]
    vel_new = (
        svel + time_step * 0.5 * (sacc + new_acc) + step_sq / 12.0 * (sjerk - new_jerk)
    )
    vel_out[...] = vel_new
    pos_out[...] = (
        spos + time_step * 0.5 * (svel + vel_new) + step_sq / 12.0 * (sacc - new_acc)
    )

    if kicks == n_wide:
        total = loop(
            n_wide * stars // ROWS, lambda g, acc: on_bodies(bodies + g * ROWS, every, acc), total
        )
    else:
        kicked = []
        for t in every:

            def one_block(k, acc):
                listed = star_leaf[t * leaves // tiles, k]
                place = listed + flip - 2 * flip * lax.rem(listed, 2)
                start = bodies + place * stars
                return loop(
                    stars // ROWS, lambda g, part: on_bodies(start + g * ROWS, (t,), part), acc
                )

            kicked.append(lax.fori_loop(0, kicks, one_block, (total[t],))[0])
        total = tuple(kicked)
    total = loop(
        n_wide * GROUPS // ROWS, lambda g, acc: on_bodies(ess_start + g * ROWS, every, acc), total
    )
    for t in every:
        for c in range(3):
            piece = jnp.sum(total[t][c], axis=0, keepdims=True)
            spot = (slice(c, c + 1), slice(t * LANES, (t + 1) * LANES))
            gal_out[spot] = gal_vel[spot] + time_step * piece

    pltpu.make_async_copy(
        states.at[pl.ds(0, n_dev - 1)], states.at[pl.ds(0, n_dev - 1)], send_sem
    ).wait()
    pltpu.make_async_copy(
        cell_out.at[pl.ds(0, n_wide - 1)], cell_out.at[pl.ds(0, n_wide - 1)], cell_send_sem
    ).wait()


def body(
    n_wide,
    n_narrow,
    star_pos,
    star_vel,
    star_mass,
    star_acc,
    star_jerk,
    gal_pos,
    gal_vel,
    gal_mass,
    group_of,
    let_send,
    star_leaf,
):
    n_dev = n_wide * n_narrow
    stars, bodies = star_pos.shape[1], gal_pos.shape[1]
    vmem = pl.BlockSpec(memory_space=pltpu.VMEM)
    smem = pl.BlockSpec(memory_space=pltpu.SMEM)
    f32 = jnp.float32
    return pl.pallas_call(
        functools.partial(kernel, n_wide, n_narrow),
        out_shape=(
            jax.ShapeDtypeStruct(gal_vel.shape, f32),
            jax.ShapeDtypeStruct(star_pos.shape, f32),
            jax.ShapeDtypeStruct(star_vel.shape, f32),
        ),
        in_specs=[vmem] * 10 + [smem],
        out_specs=(vmem,) * 3,
        scratch_shapes=[
            pltpu.VMEM((1, 4, LANES), f32),
            pltpu.VMEM((n_dev, 4, LANES), f32),
            pltpu.VMEM((n_wide, 1, LANES), f32),
            pltpu.VMEM((n_wide, 1, LANES), f32),
            pltpu.VMEM((bodies + n_wide * (stars + GROUPS), ROWS), f32),
            pltpu.VMEM((n_dev // 2, ROWS, LANES), f32),
            pltpu.VMEM((n_wide * GROUPS // LANES + 1, ROWS, LANES), f32),
            pltpu.VMEM((ROWS, LANES), f32),
            pltpu.SemaphoreType.DMA,
            pltpu.SemaphoreType.DMA,
            pltpu.SemaphoreType.DMA,
            pltpu.SemaphoreType.DMA,
        ],
        compiler_params=pltpu.CompilerParams(collective_id=0, has_side_effects=True),
    )(
        star_pos,
        star_vel,
        star_mass.reshape(1, stars),
        star_acc,
        star_jerk,
        gal_pos,
        gal_vel,
        gal_mass.reshape(1, bodies),
        group_of.reshape(1, bodies),
        let_send.reshape(n_wide, 1),
        star_leaf,
    )


def solution(mesh):
    both = ("wide", "narrow")
    columns, flat = P(None, both), P(both)
    return jax.shard_map(
        functools.partial(body, mesh.shape["wide"], mesh.shape["narrow"]),
        mesh=mesh,
        in_specs=(
            columns,
            columns,
            flat,
            columns,
            columns,
            columns,
            columns,
            flat,
            flat,
            P(both, None, None),
            P(both, None),
        ),
        out_specs=(columns, columns, columns),
        check_vma=False,
    )
```

```python
import functools

import jax
import jax.numpy as jnp
from jax import lax
from jax.experimental import pallas as pl
from jax.experimental.pallas import tpu as pltpu
from jax.sharding import PartitionSpec as P

GROUPS = 32
LANES = 128
ROWS = 8
MESH = pl.DeviceIdType.MESH

time_step = 0.25
soften_sq = 0.05


def loop(count, step, init, most=4):
    unroll = next(u for u in range(min(most, count), 0, -1) if count % u == 0)
    return lax.fori_loop(0, count, step, init, unroll=unroll)


def spread(row):
    return jnp.broadcast_to(row, (ROWS, row.shape[1]))


def column(block, index):
    return jnp.broadcast_to(block[:, index : index + 1], (ROWS, LANES))


def pull(source, mass, target, total):
    dx, dy, dz = (s - t for s, t in zip(source, target))
    inverse = lax.rsqrt(dx * dx + dy * dy + dz * dz + soften_sq)
    weight = mass * inverse * inverse * inverse
    return (total[0] + dx * weight, total[1] + dy * weight, total[2] + dz * weight)


def kernel(
    n_wide,
    n_narrow,
    star_pos_hbm,
    star_vel_hbm,
    star_mass_hbm,
    star_acc_hbm,
    star_jerk_hbm,
    gal_pos_hbm,
    gal_vel_hbm,
    gal_mass_hbm,
    group_of_hbm,
    let_send_hbm,
    star_leaf_hbm,
    out,
    star_pos,
    star_vel,
    star_mass,
    star_acc,
    star_jerk,
    gal_pos,
    gal_vel,
    gal_mass,
    group_of,
    let_send,
    star_leaf,
    in_sem,
    own,
    states,
    cell_out,
    cell_in,
    cols,
    srow,
    crow,
    send_sem,
    recv_sem,
    cell_send_sem,
    cell_recv_sem,
):
    n_dev = n_wide * n_narrow
    wide, narrow = lax.axis_index("wide"), lax.axis_index("narrow")
    me = wide * n_narrow + narrow
    stars = star_pos.shape[1]
    bodies = gal_pos.shape[1]
    leaves, kicks = star_leaf.shape
    slots = LANES // GROUPS
    step_sq = time_step * time_step

    fetches = [
        pltpu.make_async_copy(source, target, in_sem.at[i])
        for i, (source, target) in enumerate(
            (
                (star_pos_hbm, star_pos),
                (star_vel_hbm, star_vel),
                (star_mass_hbm, star_mass),
                (star_acc_hbm, star_acc),
                (star_jerk_hbm, star_jerk),
                (gal_pos_hbm, gal_pos),
                (gal_vel_hbm, gal_vel),
                (gal_mass_hbm, gal_mass),
                (group_of_hbm, group_of),
                (let_send_hbm, let_send),
                (star_leaf_hbm, star_leaf),
            )
        )
    ]
    for fetch in fetches:
        fetch.start()

    barrier = pltpu.get_barrier_semaphore()

    def greet(i, carry):
        peer = lax.rem(me + i, n_dev)
        pl.semaphore_signal(
            barrier,
            inc=1,
            device_id=(peer // n_narrow, lax.rem(peer, n_narrow)),
            device_id_type=MESH,
        )
        return carry

    lax.fori_loop(1, n_dev, greet, 0)

    lane = lax.broadcasted_iota(jnp.int32, (1, LANES), 1)
    lane4 = lax.broadcasted_iota(jnp.int32, (4, LANES), 1)
    lane8 = lax.broadcasted_iota(jnp.int32, (ROWS, LANES), 1)
    row8 = lax.broadcasted_iota(jnp.int32, (ROWS, LANES), 0)
    left = lane4 < stars

    for fetch in fetches:
        fetch.wait()

    spos, svel = star_pos[...], star_vel[...]
    sacc, sjerk = star_acc[...], star_jerk[...]
    pred_pos = (
        spos + time_step * svel + step_sq * 0.5 * sacc + step_sq * time_step / 6.0 * sjerk
    )
    pred_vel = svel + time_step * sacc + step_sq * 0.5 * sjerk
    pos4 = jnp.concatenate([pred_pos, star_mass[...]], axis=0)
    vel4 = jnp.concatenate([pred_vel, jnp.zeros((1, stars), jnp.float32)], axis=0)
    block = jnp.concatenate([pos4, vel4], axis=1)
    parity = lax.rem(wide + narrow, 2)
    block = jnp.where(parity == 0, block, pltpu.roll(block, stars, 1))
    own[0] = block
    states[me] = block
    both = jnp.concatenate([pos4, vel4], axis=0)
    targets = jnp.transpose(
        jnp.concatenate([both, jnp.zeros((ROWS, LANES - stars), jnp.float32)], axis=1)
    )

    gpos, gmass = gal_pos[...], gal_mass[...]
    body_lane = lax.broadcasted_iota(jnp.int32, (1, bodies), 1)
    segment = group_of[...] + (body_lane // (bodies // leaves)) * GROUPS
    onehot = (
        lax.broadcasted_iota(jnp.int32, (LANES, bodies), 0)
        == jnp.broadcast_to(segment, (LANES, bodies))
    ).astype(jnp.float32)
    moments = jnp.concatenate(
        [gpos * gmass, gmass, jnp.zeros((4, bodies), jnp.float32)], axis=0
    )
    sums = lax.dot_general(
        moments,
        onehot,
        (((1,), (1,)), ((), ())),
        precision=lax.Precision.HIGHEST,
        preferred_element_type=jnp.float32,
    )
    cells = jnp.where(row8 < 3, sums / spread(sums[3:4]), sums)
    crow[0] = cells

    group = lane // GROUPS
    part = jnp.bitwise_and(group - lax.rem(wide, slots), slots - 1)
    square = (n_wide, n_wide)
    diagonal = lax.broadcasted_iota(jnp.int32, square, 0) == lax.broadcasted_iota(
        jnp.int32, square, 1
    )
    listed = jnp.broadcast_to(let_send[...].astype(jnp.float32), square)
    chosen = jnp.sum(jnp.where(diagonal, listed, 0.0), axis=1, keepdims=True)
    chosen = jnp.broadcast_to(chosen, (n_wide, LANES)).astype(jnp.int32)
    outgoing = jnp.zeros((n_wide, LANES), jnp.float32)
    pick = jnp.bitwise_and(group - chosen, slots - 1)
    for k in range(slots):
        turned = cells if k == 0 else pltpu.roll(cells, k * GROUPS, 1)
        base = jnp.zeros((1, LANES), jnp.float32)
        for c in range(4):
            base = jnp.where(part == c, turned[c : c + 1], base)
        outgoing = jnp.where(
            jnp.logical_and(pick == k, chosen >= 0),
            jnp.broadcast_to(base, (n_wide, LANES)),
            outgoing,
        )
    cell_out[:, 0, :] = outgoing
    cell_in[wide] = jnp.zeros((1, LANES), jnp.float32)

    pl.semaphore_wait(barrier, n_dev - 1)

    def state_copy(peer):
        return pltpu.make_async_remote_copy(
            src_ref=own.at[0],
            dst_ref=states.at[me],
            send_sem=send_sem,
            recv_sem=recv_sem,
            device_id=(peer // n_narrow, lax.rem(peer, n_narrow)),
            device_id_type=MESH,
        )

    def cell_copy(other):
        return pltpu.make_async_remote_copy(
            src_ref=cell_out.at[other],
            dst_ref=cell_in.at[wide],
            send_sem=cell_send_sem,
            recv_sem=cell_recv_sem,
            device_id=(other, narrow),
            device_id_type=MESH,
        )

    def send_state(i, carry):
        state_copy(lax.rem(me + i, n_dev)).start()
        return carry

    def send_cell(i, carry):
        cell_copy(lax.rem(wide + i, n_wide)).start()
        return carry

    lax.fori_loop(1, n_wide, send_cell, 0)
    lax.fori_loop(1, n_dev, send_state, 0)

    tiles = bodies // LANES
    body_rows = jnp.concatenate(
        [gpos, gmass, jnp.zeros((4, bodies), jnp.float32)], axis=0
    )
    for t in range(tiles):
        cols[t * LANES : (t + 1) * LANES, :] = jnp.transpose(
            body_rows[:, t * LANES : (t + 1) * LANES]
        )
    here = [
        [spread(gpos[c : c + 1, t * LANES : (t + 1) * LANES]) for c in range(3)]
        for t in range(tiles)
    ]

    def on_bodies(start, which, total):
        source = cols[pl.ds(pl.multiple_of(start, ROWS), ROWS), :]
        place = [column(source, c) for c in range(3)]
        mass = column(source, 3)
        return tuple(pull(place, mass, here[t], total[i]) for i, t in enumerate(which))

    every = tuple(range(tiles))
    zero = jnp.zeros((ROWS, LANES), jnp.float32)
    total = tuple((zero, zero, zero) for _ in every)
    total = loop(bodies // ROWS, lambda g, acc: on_bodies(g * ROWS, every, acc), total)

    pltpu.make_async_copy(
        states.at[pl.ds(0, n_dev - 1)], states.at[pl.ds(0, n_dev - 1)], recv_sem
    ).wait()
    pltpu.make_async_copy(
        cell_in.at[pl.ds(0, n_wide - 1)], cell_in.at[pl.ds(0, n_wide - 1)], cell_recv_sem
    ).wait()

    odd = n_narrow // 2

    def star_rows(i, carry):
        w = i // odd
        first = w * n_narrow + 2 * lax.rem(i, odd)
        flip = lax.rem(w, 2)
        even_block, odd_block = states[first + flip], states[first + 1 - flip]
        srow[i, 0:4, :] = jnp.where(left, even_block, odd_block)
        srow[i, 4:8, :] = pltpu.roll(jnp.where(left, odd_block, even_block), stars, 1)
        return carry

    pairs = n_dev // 2
    loop(pairs, star_rows, 0, 16)

    flip = lax.rem(narrow, 2)

    def star_cols(i, carry):
        even_block = states[(2 * i + flip) * n_narrow + narrow]
        odd_block = states[(2 * i + 1 - flip) * n_narrow + narrow]
        rows = jnp.where(left, even_block, odd_block)
        rows = jnp.concatenate([rows, jnp.zeros((4, LANES), jnp.float32)], axis=0)
        start = pl.multiple_of(bodies + i * LANES, LANES)
        cols[pl.ds(start, LANES), :] = jnp.transpose(rows)
        return carry

    loop(n_wide // 2, star_cols, 0)

    ess_start = bodies + n_wide * stars

    def ess_rows(e, carry):
        parts = []
        for c in range(4):
            row = jnp.zeros((1, LANES), jnp.float32)
            for k in range(slots):
                row = jnp.where(group == (c + k) % slots, cell_in[e * slots + k], row)
            parts.append(row if c == 0 else pltpu.roll(row, LANES - c * GROUPS, 1))
        parts.append(jnp.zeros((4, LANES), jnp.float32))
        rows = jnp.concatenate(parts, axis=0)
        crow[e + 1] = rows
        start = pl.multiple_of(ess_start + e * LANES, LANES)
        cols[pl.ds(start, LANES), :] = jnp.transpose(rows)
        return carry

    loop(n_wide // slots, ess_rows, 0)

    pieces = []
    for t in range(0, stars, ROWS):
        mine = targets[t : t + ROWS, :]
        place = [column(mine, c) for c in range(3)]
        speed = [column(mine, 4 + c) for c in range(3)]

        def hermite(i, acc):
            rows = [spread(srow[i, c : c + 1, :]) for c in range(7)]
            dx, dy, dz = (rows[c] - place[c] for c in range(3))
            ux, uy, uz = (rows[4 + c] - speed[c] for c in range(3))
            inverse = lax.rsqrt(dx * dx + dy * dy + dz * dz + soften_sq)
            square = inverse * inverse
            weight = rows[3] * inverse * square
            approach = 3.0 * (dx * ux + dy * uy + dz * uz) * square
            return (
                acc[0] + dx * weight,
                acc[1] + dy * weight,
                acc[2] + dz * weight,
                acc[3] + (ux - dx * approach) * weight,
                acc[4] + (uy - dy * approach) * weight,
                acc[5] + (uz - dz * approach) * weight,
            )

        acc = loop(pairs, hermite, (zero,) * 6)

        def cell_pull(i, part):
            rows = [spread(crow[i, c : c + 1, :]) for c in range(4)]
            return pull(rows[:3], rows[3], place, part)

        acc = loop(n_wide // slots + 1, cell_pull, acc[:3]) + acc[3:]
        piece = jnp.zeros((ROWS, LANES), jnp.float32)
        for c in range(6):
            piece = jnp.where(lane8 == c, jnp.sum(acc[c], axis=1, keepdims=True), piece)
        pieces.append(piece)
    result = jnp.transpose(jnp.concatenate(pieces, axis=0))
    new_acc, new_jerk = result[0:3], result[3:6]
    vel_new = (
        svel + time_step * 0.5 * (sacc + new_acc) + step_sq / 12.0 * (sjerk - new_jerk)
    )
    vel_at = bodies + LANES
    out[:, vel_at : vel_at + stars] = vel_new
    out[:, bodies : bodies + stars] = (
        spos + time_step * 0.5 * (svel + vel_new) + step_sq / 12.0 * (sacc - new_acc)
    )

    if kicks == n_wide:
        total = loop(
            n_wide * stars // ROWS, lambda g, acc: on_bodies(bodies + g * ROWS, every, acc), total
        )
    else:
        kicked = []
        for t in every:

            def one_block(k, acc):
                listed = star_leaf[t * leaves // tiles, k]
                place = listed + flip - 2 * flip * lax.rem(listed, 2)
                start = bodies + place * stars
                return loop(
                    stars // ROWS, lambda g, part: on_bodies(start + g * ROWS, (t,), part), acc
                )

            kicked.append(lax.fori_loop(0, kicks, one_block, (total[t],))[0])
        total = tuple(kicked)
    total = loop(
        n_wide * GROUPS // ROWS, lambda g, acc: on_bodies(ess_start + g * ROWS, every, acc), total
    )
    for t in every:
        for c in range(3):
            piece = jnp.sum(total[t][c], axis=0, keepdims=True)
            spot = (slice(c, c + 1), slice(t * LANES, (t + 1) * LANES))
            out[spot] = gal_vel[spot] + time_step * piece

    pltpu.make_async_copy(
        states.at[pl.ds(0, n_dev - 1)], states.at[pl.ds(0, n_dev - 1)], send_sem
    ).wait()
    pltpu.make_async_copy(
        cell_out.at[pl.ds(0, n_wide - 1)], cell_out.at[pl.ds(0, n_wide - 1)], cell_send_sem
    ).wait()


def unpack(packed, gal_out, pos_out, vel_out):
    bodies, stars = gal_out.shape[1], pos_out.shape[1]
    gal_out[...] = packed[:, 0:bodies]
    pos_out[...] = packed[:, bodies : bodies + stars]
    vel_out[...] = packed[:, bodies + LANES : bodies + LANES + stars]


def body(
    n_wide,
    n_narrow,
    star_pos,
    star_vel,
    star_mass,
    star_acc,
    star_jerk,
    gal_pos,
    gal_vel,
    gal_mass,
    group_of,
    let_send,
    star_leaf,
):
    n_dev = n_wide * n_narrow
    stars, bodies = star_pos.shape[1], gal_pos.shape[1]
    vmem = pl.BlockSpec(memory_space=pltpu.VMEM)
    f32 = jnp.float32
    i32 = jnp.int32
    hbm = pl.BlockSpec(memory_space=pltpu.HBM)
    packed = pl.pallas_call(
        functools.partial(kernel, n_wide, n_narrow),
        out_shape=jax.ShapeDtypeStruct((3, bodies + 2 * LANES), f32),
        in_specs=[hbm] * 11,
        out_specs=vmem,
        scratch_shapes=[
            pltpu.VMEM((3, stars), f32),
            pltpu.VMEM((3, stars), f32),
            pltpu.VMEM((1, stars), f32),
            pltpu.VMEM((3, stars), f32),
            pltpu.VMEM((3, stars), f32),
            pltpu.VMEM((3, bodies), f32),
            pltpu.VMEM((3, bodies), f32),
            pltpu.VMEM((1, bodies), f32),
            pltpu.VMEM((1, bodies), i32),
            pltpu.VMEM((1, n_wide), i32),
            pltpu.SMEM(star_leaf.shape, i32),
            pltpu.SemaphoreType.DMA((11,)),
            pltpu.VMEM((1, 4, LANES), f32),
            pltpu.VMEM((n_dev, 4, LANES), f32),
            pltpu.VMEM((n_wide, 1, LANES), f32),
            pltpu.VMEM((n_wide, 1, LANES), f32),
            pltpu.VMEM((bodies + n_wide * (stars + GROUPS), ROWS), f32),
            pltpu.VMEM((n_dev // 2, ROWS, LANES), f32),
            pltpu.VMEM((n_wide * GROUPS // LANES + 1, ROWS, LANES), f32),
            pltpu.SemaphoreType.DMA,
            pltpu.SemaphoreType.DMA,
            pltpu.SemaphoreType.DMA,
            pltpu.SemaphoreType.DMA,
        ],
        compiler_params=pltpu.CompilerParams(
            collective_id=0, has_side_effects=True, vmem_limit_bytes=24 << 20
        ),
    )(
        *(
            pltpu.with_memory_space_constraint(array, pltpu.HBM)
            for array in (
                star_pos,
                star_vel,
                star_mass.reshape(1, stars),
                star_acc,
                star_jerk,
                gal_pos,
                gal_vel,
                gal_mass.reshape(1, bodies),
                group_of.reshape(1, bodies),
                let_send.reshape(1, n_wide),
                star_leaf,
            )
        )
    )
    return pl.pallas_call(
        unpack,
        out_shape=(
            jax.ShapeDtypeStruct(gal_vel.shape, f32),
            jax.ShapeDtypeStruct(star_pos.shape, f32),
            jax.ShapeDtypeStruct(star_vel.shape, f32),
        ),
        in_specs=[vmem],
        out_specs=(vmem,) * 3,
        compiler_params=pltpu.CompilerParams(vmem_limit_bytes=1 << 20),
    )(packed)


def solution(mesh):
    both = ("wide", "narrow")
    columns, flat = P(None, both), P(both)
    return jax.shard_map(
        functools.partial(body, mesh.shape["wide"], mesh.shape["narrow"]),
        mesh=mesh,
        in_specs=(
            columns,
            columns,
            flat,
            columns,
            columns,
            columns,
            columns,
            flat,
            flat,
            P(both, None, None),
            P(both, None),
        ),
        out_specs=(columns, columns, columns),
        check_vma=False,
    )
```

```python
import functools

import jax
import jax.numpy as jnp
from jax import lax
from jax.experimental import pallas as pl
from jax.experimental.pallas import tpu as pltpu
from jax.sharding import PartitionSpec as P

GROUPS = 32
LANES = 128
ROWS = 8
MESH = pl.DeviceIdType.MESH

time_step = 0.25
soften_sq = 0.05


def loop(count, step, init, most=4):
    unroll = next(u for u in range(min(most, count), 0, -1) if count % u == 0)
    return lax.fori_loop(0, count, step, init, unroll=unroll)


def spread(row):
    return jnp.broadcast_to(row, (ROWS, row.shape[1]))


def column(block, index):
    return jnp.broadcast_to(block[:, index : index + 1], (ROWS, LANES))


def pull(source, mass, target, total):
    dx, dy, dz = (s - t for s, t in zip(source, target))
    inverse = lax.rsqrt(dx * dx + dy * dy + dz * dz + soften_sq)
    weight = mass * inverse * inverse * inverse
    return (total[0] + dx * weight, total[1] + dy * weight, total[2] + dz * weight)


def kernel(
    n_wide,
    n_narrow,
    star_pos_hbm,
    star_vel_hbm,
    star_mass_hbm,
    star_acc_hbm,
    star_jerk_hbm,
    gal_pos_hbm,
    gal_vel_hbm,
    gal_mass_hbm,
    group_of_hbm,
    let_send_hbm,
    star_leaf_hbm,
    out,
    star_pos,
    star_vel,
    star_mass,
    star_acc,
    star_jerk,
    gal_pos,
    gal_vel,
    gal_mass,
    group_of,
    let_send,
    star_leaf,
    in_sem,
    states,
    cell_out,
    cell_in,
    cols,
    srow,
    crow,
    send_sem,
    recv_sem,
    cell_send_sem,
    cell_recv_sem,
    pass_send_sem,
    pass_recv_sem,
):
    wide, narrow = lax.axis_index("wide"), lax.axis_index("narrow")
    stars = star_pos.shape[1]
    bodies = gal_pos.shape[1]
    leaves, kicks = star_leaf.shape
    slots = LANES // GROUPS
    step_sq = time_step * time_step

    fetches = [
        pltpu.make_async_copy(source, target, in_sem.at[i])
        for i, (source, target) in enumerate(
            (
                (star_pos_hbm, star_pos),
                (star_vel_hbm, star_vel),
                (star_mass_hbm, star_mass),
                (star_acc_hbm, star_acc),
                (star_jerk_hbm, star_jerk),
                (gal_pos_hbm, gal_pos),
                (gal_vel_hbm, gal_vel),
                (gal_mass_hbm, gal_mass),
                (group_of_hbm, group_of),
                (let_send_hbm, let_send),
                (star_leaf_hbm, star_leaf),
            )
        )
    ]
    for fetch in fetches:
        fetch.start()

    barrier = pltpu.get_barrier_semaphore()

    def greet(w, n):
        pl.semaphore_signal(barrier, inc=1, device_id=(w, n), device_id_type=MESH)

    def greet_wide(i, carry):
        greet(lax.rem(wide + i, n_wide), narrow)
        return carry

    lax.fori_loop(1, n_wide, greet_wide, 0)
    for i in range(1, n_narrow):
        greet(wide, lax.rem(narrow + i, n_narrow))

    lane = lax.broadcasted_iota(jnp.int32, (1, LANES), 1)
    lane4 = lax.broadcasted_iota(jnp.int32, (4, LANES), 1)
    lane8 = lax.broadcasted_iota(jnp.int32, (ROWS, LANES), 1)
    row8 = lax.broadcasted_iota(jnp.int32, (ROWS, LANES), 0)
    left = lane4 < stars

    for fetch in fetches:
        fetch.wait()

    spos, svel = star_pos[...], star_vel[...]
    sacc, sjerk = star_acc[...], star_jerk[...]
    pred_pos = (
        spos + time_step * svel + step_sq * 0.5 * sacc + step_sq * time_step / 6.0 * sjerk
    )
    pred_vel = svel + time_step * sacc + step_sq * 0.5 * sjerk
    pos4 = jnp.concatenate([pred_pos, star_mass[...]], axis=0)
    vel4 = jnp.concatenate([pred_vel, jnp.zeros((1, stars), jnp.float32)], axis=0)
    block = jnp.concatenate([pos4, vel4], axis=1)
    block = jnp.where(lax.rem(wide, 2) == 0, block, pltpu.roll(block, stars, 1))
    states[narrow, wide] = block
    both = jnp.concatenate([pos4, vel4], axis=0)
    targets = jnp.transpose(
        jnp.concatenate([both, jnp.zeros((ROWS, LANES - stars), jnp.float32)], axis=1)
    )

    gpos, gmass = gal_pos[...], gal_mass[...]
    body_lane = lax.broadcasted_iota(jnp.int32, (1, bodies), 1)
    segment = group_of[...] + (body_lane // (bodies // leaves)) * GROUPS
    onehot = (
        lax.broadcasted_iota(jnp.int32, (LANES, bodies), 0)
        == jnp.broadcast_to(segment, (LANES, bodies))
    ).astype(jnp.float32)
    moments = jnp.concatenate(
        [gpos * gmass, gmass, jnp.zeros((4, bodies), jnp.float32)], axis=0
    )
    sums = lax.dot_general(
        moments,
        onehot,
        (((1,), (1,)), ((), ())),
        precision=lax.Precision.HIGHEST,
        preferred_element_type=jnp.float32,
    )
    cells = jnp.where(row8 < 3, sums / spread(sums[3:4]), sums)
    crow[0] = cells

    group = lane // GROUPS
    part = jnp.bitwise_and(group - lax.rem(wide, slots), slots - 1)
    square = (n_wide, n_wide)
    diagonal = lax.broadcasted_iota(jnp.int32, square, 0) == lax.broadcasted_iota(
        jnp.int32, square, 1
    )
    listed = jnp.broadcast_to(let_send[...].astype(jnp.float32), square)
    chosen = jnp.sum(jnp.where(diagonal, listed, 0.0), axis=1, keepdims=True)
    chosen = jnp.broadcast_to(chosen, (n_wide, LANES)).astype(jnp.int32)
    outgoing = jnp.zeros((n_wide, LANES), jnp.float32)
    pick = jnp.bitwise_and(group - chosen, slots - 1)
    for k in range(slots):
        turned = cells if k == 0 else pltpu.roll(cells, k * GROUPS, 1)
        base = jnp.zeros((1, LANES), jnp.float32)
        for c in range(4):
            base = jnp.where(part == c, turned[c : c + 1], base)
        outgoing = jnp.where(
            jnp.logical_and(pick == k, chosen >= 0),
            jnp.broadcast_to(base, (n_wide, LANES)),
            outgoing,
        )
    cell_out[:, 0, :] = outgoing
    cell_in[wide] = jnp.zeros((1, LANES), jnp.float32)

    pl.semaphore_wait(barrier, n_wide + n_narrow - 2)

    def send_wide(i, carry):
        peer = (lax.rem(wide + i, n_wide), narrow)
        pltpu.make_async_remote_copy(
            src_ref=states.at[narrow, wide],
            dst_ref=states.at[narrow, wide],
            send_sem=send_sem,
            recv_sem=recv_sem,
            device_id=peer,
            device_id_type=MESH,
        ).start()
        pltpu.make_async_remote_copy(
            src_ref=cell_out.at[peer[0]],
            dst_ref=cell_in.at[wide],
            send_sem=cell_send_sem,
            recv_sem=cell_recv_sem,
            device_id=peer,
            device_id_type=MESH,
        ).start()
        return carry

    lax.fori_loop(1, n_wide, send_wide, 0)

    tiles = bodies // LANES
    body_rows = jnp.concatenate(
        [gpos, gmass, jnp.zeros((4, bodies), jnp.float32)], axis=0
    )
    for t in range(tiles):
        cols[t * LANES : (t + 1) * LANES, :] = jnp.transpose(
            body_rows[:, t * LANES : (t + 1) * LANES]
        )
    here = [
        [spread(gpos[c : c + 1, t * LANES : (t + 1) * LANES]) for c in range(3)]
        for t in range(tiles)
    ]

    def on_bodies(start, which, total):
        source = cols[pl.ds(pl.multiple_of(start, ROWS), ROWS), :]
        place = [column(source, c) for c in range(3)]
        mass = column(source, 3)
        return tuple(pull(place, mass, here[t], total[i]) for i, t in enumerate(which))

    every = tuple(range(tiles))
    zero = jnp.zeros((ROWS, LANES), jnp.float32)
    total = tuple((zero, zero, zero) for _ in every)
    total = loop(bodies // ROWS, lambda g, acc: on_bodies(g * ROWS, every, acc), total)

    some = states.at[0, pl.ds(0, n_wide - 1)]
    pltpu.make_async_copy(some, some, recv_sem).wait()
    for i in range(1, n_narrow):
        pltpu.make_async_remote_copy(
            src_ref=states.at[narrow],
            dst_ref=states.at[narrow],
            send_sem=pass_send_sem,
            recv_sem=pass_recv_sem,
            device_id=(wide, lax.rem(narrow + i, n_narrow)),
            device_id_type=MESH,
        ).start()

    halves = n_wide // 2

    def star_rows(n, i):
        even_block, odd_block = states[n, 2 * i], states[n, 2 * i + 1]
        rows = jnp.where(left, even_block, odd_block)
        spot = n * halves + i
        srow[spot, 0:4, :] = rows
        srow[spot, 4:8, :] = pltpu.roll(jnp.where(left, odd_block, even_block), stars, 1)
        return rows

    def star_cols(i, carry):
        rows = jnp.concatenate(
            [star_rows(narrow, i), jnp.zeros((4, LANES), jnp.float32)], axis=0
        )
        start = pl.multiple_of(bodies + i * LANES, LANES)
        cols[pl.ds(start, LANES), :] = jnp.transpose(rows)
        return carry

    loop(halves, star_cols, 0)
    few = cell_in.at[pl.ds(0, n_wide - 1)]
    pltpu.make_async_copy(few, few, cell_recv_sem).wait()

    ess_start = bodies + n_wide * stars

    def ess_rows(e, carry):
        parts = []
        for c in range(4):
            row = jnp.zeros((1, LANES), jnp.float32)
            for k in range(slots):
                row = jnp.where(group == (c + k) % slots, cell_in[e * slots + k], row)
            parts.append(row if c == 0 else pltpu.roll(row, LANES - c * GROUPS, 1))
        parts.append(jnp.zeros((4, LANES), jnp.float32))
        rows = jnp.concatenate(parts, axis=0)
        crow[e + 1] = rows
        start = pl.multiple_of(ess_start + e * LANES, LANES)
        cols[pl.ds(start, LANES), :] = jnp.transpose(rows)
        return carry

    loop(n_wide // slots, ess_rows, 0)

    if kicks == n_wide:
        total = loop(
            n_wide * stars // ROWS, lambda g, acc: on_bodies(bodies + g * ROWS, every, acc), total
        )
    else:
        kicked = []
        for t in every:

            def one_block(k, acc):
                listed = star_leaf[t * leaves // tiles, k]
                start = bodies + listed * stars
                return loop(
                    stars // ROWS, lambda g, part: on_bodies(start + g * ROWS, (t,), part), acc
                )

            kicked.append(lax.fori_loop(0, kicks, one_block, (total[t],))[0])
        total = tuple(kicked)
    total = loop(
        n_wide * GROUPS // ROWS, lambda g, acc: on_bodies(ess_start + g * ROWS, every, acc), total
    )
    for t in every:
        for c in range(3):
            piece = jnp.sum(total[t][c], axis=0, keepdims=True)
            spot = (slice(c, c + 1), slice(t * LANES, (t + 1) * LANES))
            out[spot] = gal_vel[spot] + time_step * piece

    rest = states.at[pl.ds(0, n_narrow - 1)]
    pltpu.make_async_copy(rest, rest, pass_recv_sem).wait()

    def passed_rows(i, carry):
        n = lax.rem(narrow + 1 + i // halves, n_narrow)
        star_rows(n, lax.rem(i, halves))
        return carry

    loop((n_narrow - 1) * halves, passed_rows, 0, 12)
    pairs = n_narrow * halves

    pieces = []
    for t in range(0, stars, ROWS):
        mine = targets[t : t + ROWS, :]
        place = [column(mine, c) for c in range(3)]
        speed = [column(mine, 4 + c) for c in range(3)]

        def hermite(i, acc):
            rows = [spread(srow[i, c : c + 1, :]) for c in range(7)]
            dx, dy, dz = (rows[c] - place[c] for c in range(3))
            ux, uy, uz = (rows[4 + c] - speed[c] for c in range(3))
            inverse = lax.rsqrt(dx * dx + dy * dy + dz * dz + soften_sq)
            square = inverse * inverse
            weight = rows[3] * inverse * square
            approach = 3.0 * (dx * ux + dy * uy + dz * uz) * square
            return (
                acc[0] + dx * weight,
                acc[1] + dy * weight,
                acc[2] + dz * weight,
                acc[3] + (ux - dx * approach) * weight,
                acc[4] + (uy - dy * approach) * weight,
                acc[5] + (uz - dz * approach) * weight,
            )

        acc = loop(pairs, hermite, (zero,) * 6)

        def cell_pull(i, part):
            rows = [spread(crow[i, c : c + 1, :]) for c in range(4)]
            return pull(rows[:3], rows[3], place, part)

        acc = loop(n_wide // slots + 1, cell_pull, acc[:3]) + acc[3:]
        piece = jnp.zeros((ROWS, LANES), jnp.float32)
        for c in range(6):
            piece = jnp.where(lane8 == c, jnp.sum(acc[c], axis=1, keepdims=True), piece)
        pieces.append(piece)
    result = jnp.transpose(jnp.concatenate(pieces, axis=0))
    new_acc, new_jerk = result[0:3], result[3:6]
    vel_new = (
        svel + time_step * 0.5 * (sacc + new_acc) + step_sq / 12.0 * (sjerk - new_jerk)
    )
    vel_at = bodies + LANES
    out[:, vel_at : vel_at + stars] = vel_new
    out[:, bodies : bodies + stars] = (
        spos + time_step * 0.5 * (svel + vel_new) + step_sq / 12.0 * (sacc - new_acc)
    )

    pltpu.make_async_copy(some, some, send_sem).wait()
    pltpu.make_async_copy(few, few, cell_send_sem).wait()
    pltpu.make_async_copy(rest, rest, pass_send_sem).wait()


def unpack(packed, gal_out, pos_out, vel_out):
    bodies, stars = gal_out.shape[1], pos_out.shape[1]
    gal_out[...] = packed[:, 0:bodies]
    pos_out[...] = packed[:, bodies : bodies + stars]
    vel_out[...] = packed[:, bodies + LANES : bodies + LANES + stars]


def body(
    n_wide,
    n_narrow,
    star_pos,
    star_vel,
    star_mass,
    star_acc,
    star_jerk,
    gal_pos,
    gal_vel,
    gal_mass,
    group_of,
    let_send,
    star_leaf,
):
    n_dev = n_wide * n_narrow
    stars, bodies = star_pos.shape[1], gal_pos.shape[1]
    vmem = pl.BlockSpec(memory_space=pltpu.VMEM)
    f32 = jnp.float32
    i32 = jnp.int32
    hbm = pl.BlockSpec(memory_space=pltpu.HBM)
    packed = pl.pallas_call(
        functools.partial(kernel, n_wide, n_narrow),
        out_shape=jax.ShapeDtypeStruct((3, bodies + 2 * LANES), f32),
        in_specs=[hbm] * 11,
        out_specs=vmem,
        scratch_shapes=[
            pltpu.VMEM((3, stars), f32),
            pltpu.VMEM((3, stars), f32),
            pltpu.VMEM((1, stars), f32),
            pltpu.VMEM((3, stars), f32),
            pltpu.VMEM((3, stars), f32),
            pltpu.VMEM((3, bodies), f32),
            pltpu.VMEM((3, bodies), f32),
            pltpu.VMEM((1, bodies), f32),
            pltpu.VMEM((1, bodies), i32),
            pltpu.VMEM((1, n_wide), i32),
            pltpu.SMEM(star_leaf.shape, i32),
            pltpu.SemaphoreType.DMA((11,)),
            pltpu.VMEM((n_narrow, n_wide, 4, LANES), f32),
            pltpu.VMEM((n_wide, 1, LANES), f32),
            pltpu.VMEM((n_wide, 1, LANES), f32),
            pltpu.VMEM((bodies + n_wide * (stars + GROUPS), ROWS), f32),
            pltpu.VMEM((n_dev // 2, ROWS, LANES), f32),
            pltpu.VMEM((n_wide * GROUPS // LANES + 1, ROWS, LANES), f32),
            pltpu.SemaphoreType.DMA,
            pltpu.SemaphoreType.DMA,
            pltpu.SemaphoreType.DMA,
            pltpu.SemaphoreType.DMA,
            pltpu.SemaphoreType.DMA,
            pltpu.SemaphoreType.DMA,
        ],
        compiler_params=pltpu.CompilerParams(
            collective_id=0, has_side_effects=True, vmem_limit_bytes=24 << 20
        ),
    )(
        *(
            pltpu.with_memory_space_constraint(array, pltpu.HBM)
            for array in (
                star_pos,
                star_vel,
                star_mass.reshape(1, stars),
                star_acc,
                star_jerk,
                gal_pos,
                gal_vel,
                gal_mass.reshape(1, bodies),
                group_of.reshape(1, bodies),
                let_send.reshape(1, n_wide),
                star_leaf,
            )
        )
    )
    return pl.pallas_call(
        unpack,
        out_shape=(
            jax.ShapeDtypeStruct(gal_vel.shape, f32),
            jax.ShapeDtypeStruct(star_pos.shape, f32),
            jax.ShapeDtypeStruct(star_vel.shape, f32),
        ),
        in_specs=[vmem],
        out_specs=(vmem,) * 3,
        compiler_params=pltpu.CompilerParams(vmem_limit_bytes=1 << 20),
    )(packed)


def solution(mesh):
    both = ("wide", "narrow")
    columns, flat = P(None, both), P(both)
    return jax.shard_map(
        functools.partial(body, mesh.shape["wide"], mesh.shape["narrow"]),
        mesh=mesh,
        in_specs=(
            columns,
            columns,
            flat,
            columns,
            columns,
            columns,
            columns,
            flat,
            flat,
            P(both, None, None),
            P(both, None),
        ),
        out_specs=(columns, columns, columns),
        check_vma=False,
    )
```

```python
import functools

import jax
import jax.numpy as jnp
from jax import lax
from jax.experimental import pallas as pl
from jax.experimental.pallas import tpu as pltpu
from jax.sharding import PartitionSpec as P

GROUPS = 32
LANES = 128
ROWS = 8
BODY_UNROLL = 16
STAR_UNROLL = 16
MESH = pl.DeviceIdType.MESH

time_step = 0.25
soften_sq = 0.05


def loop(count, step, init, most=4):
    unroll = next(u for u in range(min(most, count), 0, -1) if count % u == 0)
    return lax.fori_loop(0, count, step, init, unroll=unroll)


def spread(row):
    return jnp.broadcast_to(row, (ROWS, row.shape[1]))


def column(block, index):
    return jnp.broadcast_to(block[:, index : index + 1], (ROWS, LANES))


def pull(source, mass, target, total):
    dx, dy, dz = (s - t for s, t in zip(source, target))
    inverse = lax.rsqrt(dx * dx + dy * dy + dz * dz + soften_sq)
    weight = mass * inverse * inverse * inverse
    return (total[0] + dx * weight, total[1] + dy * weight, total[2] + dz * weight)


def kernel(
    n_wide,
    n_narrow,
    star_pos_hbm,
    star_vel_hbm,
    star_mass_hbm,
    star_acc_hbm,
    star_jerk_hbm,
    gal_pos_hbm,
    gal_vel_hbm,
    gal_mass_hbm,
    group_of_hbm,
    let_send_hbm,
    star_leaf_hbm,
    out,
    star_pos,
    star_vel,
    star_mass,
    star_acc,
    star_jerk,
    gal_pos,
    gal_vel,
    gal_mass,
    group_of,
    let_send,
    star_leaf,
    in_sem,
    states,
    cell_out,
    cell_in,
    cols,
    srow,
    crow,
    send_sem,
    recv_sem,
    cell_send_sem,
    cell_recv_sem,
    pass_send_sem,
    pass_recv_sem,
):
    wide, narrow = lax.axis_index("wide"), lax.axis_index("narrow")
    stars = star_pos.shape[1]
    bodies = gal_pos.shape[1]
    leaves, kicks = star_leaf.shape
    slots = LANES // GROUPS
    step_sq = time_step * time_step

    fetches = [
        pltpu.make_async_copy(source, target, in_sem.at[i])
        for i, (source, target) in enumerate(
            (
                (star_pos_hbm, star_pos),
                (star_vel_hbm, star_vel),
                (star_mass_hbm, star_mass),
                (star_acc_hbm, star_acc),
                (star_jerk_hbm, star_jerk),
                (gal_pos_hbm, gal_pos),
                (gal_vel_hbm, gal_vel),
                (gal_mass_hbm, gal_mass),
                (group_of_hbm, group_of),
                (let_send_hbm, let_send),
                (star_leaf_hbm, star_leaf),
            )
        )
    ]
    for fetch in fetches:
        fetch.start()

    barrier = pltpu.get_barrier_semaphore()

    def greet(w, n):
        pl.semaphore_signal(barrier, inc=1, device_id=(w, n), device_id_type=MESH)

    beside = [narrow] + [lax.rem(narrow + m, n_narrow) for m in range(1, n_narrow)]

    def each_wide(first, step):
        lax.fori_loop(first, n_wide, step, 0, unroll=n_wide <= 16)

    def greet_peers(j, carry):
        w = lax.rem(wide + j, n_wide)
        for n in beside:
            greet(w, n)
        return carry

    each_wide(1, greet_peers)
    for n in beside[1:]:
        greet(wide, n)

    lane = lax.broadcasted_iota(jnp.int32, (1, LANES), 1)
    lane4 = lax.broadcasted_iota(jnp.int32, (4, LANES), 1)
    lane8 = lax.broadcasted_iota(jnp.int32, (ROWS, LANES), 1)
    row8 = lax.broadcasted_iota(jnp.int32, (ROWS, LANES), 0)
    left = lane4 < stars

    for fetch in fetches:
        fetch.wait()

    spos, svel = star_pos[...], star_vel[...]
    sacc, sjerk = star_acc[...], star_jerk[...]
    pred_pos = (
        spos + time_step * svel + step_sq * 0.5 * sacc + step_sq * time_step / 6.0 * sjerk
    )
    pred_vel = svel + time_step * sacc + step_sq * 0.5 * sjerk
    pos4 = jnp.concatenate([pred_pos, star_mass[...]], axis=0)
    vel4 = jnp.concatenate([pred_vel, jnp.zeros((1, stars), jnp.float32)], axis=0)
    block = jnp.concatenate([pos4, vel4], axis=1)
    block = jnp.where(lax.rem(wide, 2) == 0, block, pltpu.roll(block, stars, 1))
    states[narrow, wide] = block
    both = jnp.concatenate([pos4, vel4], axis=0)
    targets = jnp.transpose(
        jnp.concatenate([both, jnp.zeros((ROWS, LANES - stars), jnp.float32)], axis=1)
    )

    gpos, gmass = gal_pos[...], gal_mass[...]
    body_lane = lax.broadcasted_iota(jnp.int32, (1, bodies), 1)
    segment = group_of[...] + (body_lane // (bodies // leaves)) * GROUPS
    onehot = (
        lax.broadcasted_iota(jnp.int32, (LANES, bodies), 0)
        == jnp.broadcast_to(segment, (LANES, bodies))
    ).astype(jnp.float32)
    moments = jnp.concatenate(
        [gpos * gmass, gmass, jnp.zeros((4, bodies), jnp.float32)], axis=0
    )
    sums = lax.dot_general(
        moments,
        onehot,
        (((1,), (1,)), ((), ())),
        precision=lax.Precision.HIGHEST,
        preferred_element_type=jnp.float32,
    )
    cells = jnp.where(row8 < 3, sums / spread(sums[3:4]), sums)
    crow[0] = cells

    group = lane // GROUPS
    part = jnp.bitwise_and(group - lax.rem(wide, slots), slots - 1)
    square = (n_wide, n_wide)
    diagonal = lax.broadcasted_iota(jnp.int32, square, 0) == lax.broadcasted_iota(
        jnp.int32, square, 1
    )
    listed = jnp.broadcast_to(let_send[...].astype(jnp.float32), square)
    chosen = jnp.sum(jnp.where(diagonal, listed, 0.0), axis=1, keepdims=True)
    chosen = jnp.broadcast_to(chosen, (n_wide, LANES)).astype(jnp.int32)
    outgoing = jnp.zeros((n_wide, LANES), jnp.float32)
    pick = jnp.bitwise_and(group - chosen, slots - 1)
    for k in range(slots):
        turned = cells if k == 0 else pltpu.roll(cells, k * GROUPS, 1)
        base = jnp.zeros((1, LANES), jnp.float32)
        for c in range(4):
            base = jnp.where(part == c, turned[c : c + 1], base)
        outgoing = jnp.where(
            jnp.logical_and(pick == k, chosen >= 0),
            jnp.broadcast_to(base, (n_wide, LANES)),
            outgoing,
        )
    cell_out[:, 0, :] = outgoing
    cell_in[wide] = jnp.zeros((1, LANES), jnp.float32)

    pl.semaphore_wait(barrier, n_wide * n_narrow - 1)

    def send_state(w, n, sends, recvs):
        pltpu.make_async_remote_copy(
            src_ref=states.at[narrow, wide],
            dst_ref=states.at[narrow, wide],
            send_sem=sends,
            recv_sem=recvs,
            device_id=(w, n),
            device_id_type=MESH,
        ).start()

    def send_wide(j, carry):
        w = lax.rem(wide + j, n_wide)
        pltpu.make_async_remote_copy(
            src_ref=cell_out.at[w],
            dst_ref=cell_in.at[wide],
            send_sem=cell_send_sem,
            recv_sem=cell_recv_sem,
            device_id=(w, narrow),
            device_id_type=MESH,
        ).start()
        send_state(w, narrow, send_sem, recv_sem)
        return carry

    def send_others(j, carry):
        w = lax.rem(wide + j, n_wide)
        for n in beside[1:]:
            send_state(w, n, pass_send_sem, pass_recv_sem)
        return carry

    each_wide(1, send_wide)
    each_wide(1, send_others)
    for n in beside[1:]:
        send_state(wide, n, pass_send_sem, pass_recv_sem)

    tiles = bodies // LANES
    body_rows = jnp.concatenate(
        [gpos, gmass, jnp.zeros((4, bodies), jnp.float32)], axis=0
    )
    for t in range(tiles):
        cols[t * LANES : (t + 1) * LANES, :] = jnp.transpose(
            body_rows[:, t * LANES : (t + 1) * LANES]
        )
    here = [
        [spread(gpos[c : c + 1, t * LANES : (t + 1) * LANES]) for c in range(3)]
        for t in range(tiles)
    ]

    def on_bodies(start, which, total):
        source = cols[pl.ds(pl.multiple_of(start, ROWS), ROWS), :]
        place = [column(source, c) for c in range(3)]
        mass = column(source, 3)
        return tuple(pull(place, mass, here[t], total[i]) for i, t in enumerate(which))

    every = tuple(range(tiles))
    zero = jnp.zeros((ROWS, LANES), jnp.float32)
    total = tuple((zero, zero, zero) for _ in every)
    total = loop(bodies // ROWS, lambda g, acc: on_bodies(g * ROWS, every, acc), total, BODY_UNROLL)

    some = states.at[0, pl.ds(0, n_wide - 1)]
    pltpu.make_async_copy(some, some, recv_sem).wait()
    halves = n_wide // 2

    def star_rows(n, i):
        even_block, odd_block = states[n, 2 * i], states[n, 2 * i + 1]
        rows = jnp.where(left, even_block, odd_block)
        spot = n * halves + i
        srow[spot, 0:4, :] = rows
        srow[spot, 4:8, :] = pltpu.roll(jnp.where(left, odd_block, even_block), stars, 1)
        return rows

    def star_cols(i, carry):
        rows = jnp.concatenate(
            [star_rows(narrow, i), jnp.zeros((4, LANES), jnp.float32)], axis=0
        )
        start = pl.multiple_of(bodies + i * LANES, LANES)
        cols[pl.ds(start, LANES), :] = jnp.transpose(rows)
        return carry

    loop(halves, star_cols, 0)
    few = cell_in.at[pl.ds(0, n_wide - 1)]
    pltpu.make_async_copy(few, few, cell_recv_sem).wait()

    ess_start = bodies + n_wide * stars

    def ess_rows(e, carry):
        parts = []
        for c in range(4):
            row = jnp.zeros((1, LANES), jnp.float32)
            for k in range(slots):
                row = jnp.where(group == (c + k) % slots, cell_in[e * slots + k], row)
            parts.append(row if c == 0 else pltpu.roll(row, LANES - c * GROUPS, 1))
        parts.append(jnp.zeros((4, LANES), jnp.float32))
        rows = jnp.concatenate(parts, axis=0)
        crow[e + 1] = rows
        start = pl.multiple_of(ess_start + e * LANES, LANES)
        cols[pl.ds(start, LANES), :] = jnp.transpose(rows)
        return carry

    loop(n_wide // slots, ess_rows, 0)

    if kicks == n_wide:
        shared = bodies
    else:
        shared = ess_start
        kicked = []
        for t in every:

            def one_block(k, acc):
                listed = star_leaf[t * leaves // tiles, k]
                start = bodies + listed * stars
                return loop(
                    stars // ROWS, lambda g, part: on_bodies(start + g * ROWS, (t,), part), acc
                )

            kicked.append(lax.fori_loop(0, kicks, one_block, (total[t],))[0])
        total = tuple(kicked)
    total = loop(
        (ess_start + n_wide * GROUPS - shared) // ROWS,
        lambda g, acc: on_bodies(shared + g * ROWS, every, acc),
        total,
        BODY_UNROLL,
    )
    for t in every:
        for c in range(3):
            piece = jnp.sum(total[t][c], axis=0, keepdims=True)
            spot = (slice(c, c + 1), slice(t * LANES, (t + 1) * LANES))
            out[spot] = gal_vel[spot] + time_step * piece

    rest = states.at[pl.ds(0, n_narrow - 1)]
    pltpu.make_async_copy(rest, rest, pass_recv_sem).wait()

    def passed_rows(i, carry):
        n = lax.rem(narrow + 1 + i // halves, n_narrow)
        star_rows(n, lax.rem(i, halves))
        return carry

    loop((n_narrow - 1) * halves, passed_rows, 0, 12)
    pairs = n_narrow * halves

    pieces = []
    for t in range(0, stars, ROWS):
        mine = targets[t : t + ROWS, :]
        place = [column(mine, c) for c in range(3)]
        speed = [column(mine, 4 + c) for c in range(3)]

        def hermite(i, acc):
            rows = [spread(srow[i, c : c + 1, :]) for c in range(7)]
            dx, dy, dz = (rows[c] - place[c] for c in range(3))
            ux, uy, uz = (rows[4 + c] - speed[c] for c in range(3))
            inverse = lax.rsqrt(dx * dx + dy * dy + dz * dz + soften_sq)
            square = inverse * inverse
            weight = rows[3] * inverse * square
            approach = 3.0 * (dx * ux + dy * uy + dz * uz) * square
            return (
                acc[0] + dx * weight,
                acc[1] + dy * weight,
                acc[2] + dz * weight,
                acc[3] + (ux - dx * approach) * weight,
                acc[4] + (uy - dy * approach) * weight,
                acc[5] + (uz - dz * approach) * weight,
            )

        acc = loop(pairs, hermite, (zero,) * 6, STAR_UNROLL)

        def cell_pull(i, part):
            rows = [spread(crow[i, c : c + 1, :]) for c in range(4)]
            return pull(rows[:3], rows[3], place, part)

        acc = loop(n_wide // slots + 1, cell_pull, acc[:3]) + acc[3:]
        piece = jnp.zeros((ROWS, LANES), jnp.float32)
        for c in range(6):
            piece = jnp.where(lane8 == c, jnp.sum(acc[c], axis=1, keepdims=True), piece)
        pieces.append(piece)
    result = jnp.transpose(jnp.concatenate(pieces, axis=0))
    new_acc, new_jerk = result[0:3], result[3:6]
    vel_new = (
        svel + time_step * 0.5 * (sacc + new_acc) + step_sq / 12.0 * (sjerk - new_jerk)
    )
    vel_at = bodies + LANES
    out[:, vel_at : vel_at + stars] = vel_new
    out[:, bodies : bodies + stars] = (
        spos + time_step * 0.5 * (svel + vel_new) + step_sq / 12.0 * (sacc - new_acc)
    )

    pltpu.make_async_copy(some, some, send_sem).wait()
    pltpu.make_async_copy(few, few, cell_send_sem).wait()
    pltpu.make_async_copy(rest, rest, pass_send_sem).wait()


def unpack(packed, gal_out, pos_out, vel_out):
    bodies, stars = gal_out.shape[1], pos_out.shape[1]
    gal_out[...] = packed[:, 0:bodies]
    pos_out[...] = packed[:, bodies : bodies + stars]
    vel_out[...] = packed[:, bodies + LANES : bodies + LANES + stars]


def body(
    n_wide,
    n_narrow,
    star_pos,
    star_vel,
    star_mass,
    star_acc,
    star_jerk,
    gal_pos,
    gal_vel,
    gal_mass,
    group_of,
    let_send,
    star_leaf,
):
    n_dev = n_wide * n_narrow
    stars, bodies = star_pos.shape[1], gal_pos.shape[1]
    vmem = pl.BlockSpec(memory_space=pltpu.VMEM)
    f32 = jnp.float32
    i32 = jnp.int32
    hbm = pl.BlockSpec(memory_space=pltpu.HBM)
    packed = pl.pallas_call(
        functools.partial(kernel, n_wide, n_narrow),
        out_shape=jax.ShapeDtypeStruct((3, bodies + 2 * LANES), f32),
        in_specs=[hbm] * 11,
        out_specs=vmem,
        scratch_shapes=[
            pltpu.VMEM((3, stars), f32),
            pltpu.VMEM((3, stars), f32),
            pltpu.VMEM((1, stars), f32),
            pltpu.VMEM((3, stars), f32),
            pltpu.VMEM((3, stars), f32),
            pltpu.VMEM((3, bodies), f32),
            pltpu.VMEM((3, bodies), f32),
            pltpu.VMEM((1, bodies), f32),
            pltpu.VMEM((1, bodies), i32),
            pltpu.VMEM((1, n_wide), i32),
            pltpu.SMEM(star_leaf.shape, i32),
            pltpu.SemaphoreType.DMA((11,)),
            pltpu.VMEM((n_narrow, n_wide, 4, LANES), f32),
            pltpu.VMEM((n_wide, 1, LANES), f32),
            pltpu.VMEM((n_wide, 1, LANES), f32),
            pltpu.VMEM((bodies + n_wide * (stars + GROUPS), ROWS), f32),
            pltpu.VMEM((n_dev // 2, ROWS, LANES), f32),
            pltpu.VMEM((n_wide * GROUPS // LANES + 1, ROWS, LANES), f32),
            pltpu.SemaphoreType.DMA,
            pltpu.SemaphoreType.DMA,
            pltpu.SemaphoreType.DMA,
            pltpu.SemaphoreType.DMA,
            pltpu.SemaphoreType.DMA,
            pltpu.SemaphoreType.DMA,
        ],
        compiler_params=pltpu.CompilerParams(
            collective_id=0, has_side_effects=True, vmem_limit_bytes=24 << 20
        ),
    )(
        *(
            pltpu.with_memory_space_constraint(array, pltpu.HBM)
            for array in (
                star_pos,
                star_vel,
                star_mass.reshape(1, stars),
                star_acc,
                star_jerk,
                gal_pos,
                gal_vel,
                gal_mass.reshape(1, bodies),
                group_of.reshape(1, bodies),
                let_send.reshape(1, n_wide),
                star_leaf,
            )
        )
    )
    return pl.pallas_call(
        unpack,
        out_shape=(
            jax.ShapeDtypeStruct(gal_vel.shape, f32),
            jax.ShapeDtypeStruct(star_pos.shape, f32),
            jax.ShapeDtypeStruct(star_vel.shape, f32),
        ),
        in_specs=[vmem],
        out_specs=(vmem,) * 3,
        compiler_params=pltpu.CompilerParams(vmem_limit_bytes=1 << 20),
    )(packed)


def solution(mesh):
    both = ("wide", "narrow")
    columns, flat = P(None, both), P(both)
    return jax.shard_map(
        functools.partial(body, mesh.shape["wide"], mesh.shape["narrow"]),
        mesh=mesh,
        in_specs=(
            columns,
            columns,
            flat,
            columns,
            columns,
            columns,
            columns,
            flat,
            flat,
            P(both, None, None),
            P(both, None),
        ),
        out_specs=(columns, columns, columns),
        check_vma=False,
    )
```

```python
import functools

import jax
import jax.numpy as jnp
from jax import lax
from jax.experimental import pallas as pl
from jax.experimental.pallas import tpu as pltpu
from jax.sharding import PartitionSpec as P

GROUPS = 32
LANES = 128
ROWS = 8
BODY_UNROLL = 32
STAR_UNROLL = 16
MESH = pl.DeviceIdType.MESH

time_step = 0.25
soften_sq = 0.05


def loop(count, step, init, most=4):
    unroll = next(u for u in range(min(most, count), 0, -1) if count % u == 0)
    return lax.fori_loop(0, count, step, init, unroll=unroll)


def spread(row):
    return jnp.broadcast_to(row, (ROWS, row.shape[1]))


def column(block, index):
    return jnp.broadcast_to(block[:, index : index + 1], (ROWS, LANES))


def pull(source, mass, target, total):
    dx, dy, dz = (s - t for s, t in zip(source, target))
    inverse = lax.rsqrt(dx * dx + dy * dy + dz * dz + soften_sq)
    weight = mass * inverse * inverse * inverse
    return (total[0] + dx * weight, total[1] + dy * weight, total[2] + dz * weight)


def kernel(
    n_wide,
    n_narrow,
    star_pos_hbm,
    star_vel_hbm,
    star_mass_hbm,
    star_acc_hbm,
    star_jerk_hbm,
    gal_pos_hbm,
    gal_vel_hbm,
    gal_mass_hbm,
    group_of_hbm,
    let_send_hbm,
    star_leaf_hbm,
    out,
    star_pos,
    star_vel,
    star_mass,
    star_acc,
    star_jerk,
    gal_pos,
    gal_vel,
    gal_mass,
    group_of,
    let_send,
    star_leaf,
    in_sem,
    states,
    cell_out,
    cell_in,
    cols,
    srow,
    crow,
    send_sem,
    recv_sem,
    cell_send_sem,
    cell_recv_sem,
    pass_send_sem,
    pass_recv_sem,
):
    wide, narrow = lax.axis_index("wide"), lax.axis_index("narrow")
    stars = star_pos.shape[1]
    bodies = gal_pos.shape[1]
    leaves, kicks = star_leaf.shape
    slots = LANES // GROUPS
    step_sq = time_step * time_step

    fetches = [
        pltpu.make_async_copy(source, target, in_sem.at[i])
        for i, (source, target) in enumerate(
            (
                (star_pos_hbm, star_pos),
                (star_vel_hbm, star_vel),
                (star_mass_hbm, star_mass),
                (star_acc_hbm, star_acc),
                (star_jerk_hbm, star_jerk),
                (gal_pos_hbm, gal_pos),
                (gal_vel_hbm, gal_vel),
                (gal_mass_hbm, gal_mass),
                (group_of_hbm, group_of),
                (let_send_hbm, let_send),
                (star_leaf_hbm, star_leaf),
            )
        )
    ]
    barrier = pltpu.get_barrier_semaphore()

    def greet(w, n):
        pl.semaphore_signal(barrier, inc=1, device_id=(w, n), device_id_type=MESH)

    beside = [narrow] + [lax.rem(narrow + m, n_narrow) for m in range(1, n_narrow)]

    def each_wide(first, step):
        lax.fori_loop(first, n_wide, step, 0, unroll=n_wide <= 16)

    def greet_peers(j, carry):
        w = lax.rem(wide + j, n_wide)
        for n in beside:
            greet(w, n)
        return carry

    each_wide(1, greet_peers)
    for n in beside[1:]:
        greet(wide, n)

    for fetch in fetches:
        fetch.start()

    lane = lax.broadcasted_iota(jnp.int32, (1, LANES), 1)
    lane4 = lax.broadcasted_iota(jnp.int32, (4, LANES), 1)
    lane8 = lax.broadcasted_iota(jnp.int32, (ROWS, LANES), 1)
    row8 = lax.broadcasted_iota(jnp.int32, (ROWS, LANES), 0)
    left = lane4 < stars

    for fetch in fetches:
        fetch.wait()

    spos, svel = star_pos[...], star_vel[...]
    sacc, sjerk = star_acc[...], star_jerk[...]
    pred_pos = (
        spos + time_step * svel + step_sq * 0.5 * sacc + step_sq * time_step / 6.0 * sjerk
    )
    pred_vel = svel + time_step * sacc + step_sq * 0.5 * sjerk
    pos4 = jnp.concatenate([pred_pos, star_mass[...]], axis=0)
    vel4 = jnp.concatenate([pred_vel, jnp.zeros((1, stars), jnp.float32)], axis=0)
    block = jnp.concatenate([pos4, vel4], axis=1)
    block = jnp.where(lax.rem(wide, 2) == 0, block, pltpu.roll(block, stars, 1))
    states[narrow, wide] = block
    both = jnp.concatenate([pos4, vel4], axis=0)
    targets = jnp.transpose(
        jnp.concatenate([both, jnp.zeros((ROWS, LANES - stars), jnp.float32)], axis=1)
    )

    gpos, gmass = gal_pos[...], gal_mass[...]
    body_lane = lax.broadcasted_iota(jnp.int32, (1, bodies), 1)
    segment = group_of[...] + (body_lane // (bodies // leaves)) * GROUPS
    onehot = (
        lax.broadcasted_iota(jnp.int32, (LANES, bodies), 0)
        == jnp.broadcast_to(segment, (LANES, bodies))
    ).astype(jnp.float32)
    moments = jnp.concatenate(
        [gpos * gmass, gmass, jnp.zeros((4, bodies), jnp.float32)], axis=0
    )
    sums = lax.dot_general(
        moments,
        onehot,
        (((1,), (1,)), ((), ())),
        precision=lax.Precision.HIGHEST,
        preferred_element_type=jnp.float32,
    )
    cells = jnp.where(row8 < 3, sums / spread(sums[3:4]), sums)
    crow[0] = cells

    group = lane // GROUPS
    part = jnp.bitwise_and(group - lax.rem(wide, slots), slots - 1)
    square = (n_wide, n_wide)
    diagonal = lax.broadcasted_iota(jnp.int32, square, 0) == lax.broadcasted_iota(
        jnp.int32, square, 1
    )
    listed = jnp.broadcast_to(let_send[...].astype(jnp.float32), square)
    chosen = jnp.sum(jnp.where(diagonal, listed, 0.0), axis=1, keepdims=True)
    chosen = jnp.broadcast_to(chosen, (n_wide, LANES)).astype(jnp.int32)
    outgoing = jnp.zeros((n_wide, LANES), jnp.float32)
    pick = jnp.bitwise_and(group - chosen, slots - 1)
    for k in range(slots):
        turned = cells if k == 0 else pltpu.roll(cells, k * GROUPS, 1)
        base = jnp.zeros((1, LANES), jnp.float32)
        for c in range(4):
            base = jnp.where(part == c, turned[c : c + 1], base)
        outgoing = jnp.where(
            jnp.logical_and(pick == k, chosen >= 0),
            jnp.broadcast_to(base, (n_wide, LANES)),
            outgoing,
        )
    cell_out[:, 0, :] = outgoing
    cell_in[wide] = jnp.zeros((1, LANES), jnp.float32)

    pl.semaphore_wait(barrier, n_wide * n_narrow - 1)

    def send_state(w, n, sends, recvs):
        pltpu.make_async_remote_copy(
            src_ref=states.at[narrow, wide],
            dst_ref=states.at[narrow, wide],
            send_sem=sends,
            recv_sem=recvs,
            device_id=(w, n),
            device_id_type=MESH,
        ).start()

    def send_wide(j, carry):
        w = lax.rem(wide + j, n_wide)
        pltpu.make_async_remote_copy(
            src_ref=cell_out.at[w],
            dst_ref=cell_in.at[wide],
            send_sem=cell_send_sem,
            recv_sem=cell_recv_sem,
            device_id=(w, narrow),
            device_id_type=MESH,
        ).start()
        send_state(w, narrow, send_sem, recv_sem)
        return carry

    def send_others(j, carry):
        w = lax.rem(wide + j, n_wide)
        for n in beside[1:]:
            send_state(w, n, pass_send_sem, pass_recv_sem)
        return carry

    each_wide(1, send_wide)
    each_wide(1, send_others)
    for n in beside[1:]:
        send_state(wide, n, pass_send_sem, pass_recv_sem)

    tiles = bodies // LANES
    body_rows = jnp.concatenate(
        [gpos, gmass, jnp.zeros((4, bodies), jnp.float32)], axis=0
    )
    for t in range(tiles):
        cols[t * LANES : (t + 1) * LANES, :] = jnp.transpose(
            body_rows[:, t * LANES : (t + 1) * LANES]
        )
    here = [
        [spread(gpos[c : c + 1, t * LANES : (t + 1) * LANES]) for c in range(3)]
        for t in range(tiles)
    ]

    def on_bodies(start, which, total):
        source = cols[pl.ds(pl.multiple_of(start, ROWS), ROWS), :]
        place = [column(source, c) for c in range(3)]
        mass = column(source, 3)
        return tuple(pull(place, mass, here[t], total[i]) for i, t in enumerate(which))

    every = tuple(range(tiles))
    zero = jnp.zeros((ROWS, LANES), jnp.float32)
    total = tuple((zero, zero, zero) for _ in every)
    total = loop(bodies // ROWS, lambda g, acc: on_bodies(g * ROWS, every, acc), total, BODY_UNROLL)

    some = states.at[0, pl.ds(0, n_wide - 1)]
    pltpu.make_async_copy(some, some, recv_sem).wait()
    few = cell_in.at[pl.ds(0, n_wide - 1)]
    pltpu.make_async_copy(few, few, cell_recv_sem).wait()
    halves = n_wide // 2

    def star_rows(n, i):
        even_block, odd_block = states[n, 2 * i], states[n, 2 * i + 1]
        rows = jnp.where(left, even_block, odd_block)
        spot = n * halves + i
        srow[spot, 0:4, :] = rows
        srow[spot, 4:8, :] = pltpu.roll(jnp.where(left, odd_block, even_block), stars, 1)
        return rows

    def star_cols(i, carry):
        rows = jnp.concatenate(
            [star_rows(narrow, i), jnp.zeros((4, LANES), jnp.float32)], axis=0
        )
        start = pl.multiple_of(bodies + i * LANES, LANES)
        cols[pl.ds(start, LANES), :] = jnp.transpose(rows)
        return carry

    loop(halves, star_cols, 0)
    ess_start = bodies + n_wide * stars

    def ess_rows(e, carry):
        parts = []
        for c in range(4):
            row = jnp.zeros((1, LANES), jnp.float32)
            for k in range(slots):
                row = jnp.where(group == (c + k) % slots, cell_in[e * slots + k], row)
            parts.append(row if c == 0 else pltpu.roll(row, LANES - c * GROUPS, 1))
        parts.append(jnp.zeros((4, LANES), jnp.float32))
        rows = jnp.concatenate(parts, axis=0)
        crow[e + 1] = rows
        start = pl.multiple_of(ess_start + e * LANES, LANES)
        cols[pl.ds(start, LANES), :] = jnp.transpose(rows)
        return carry

    loop(n_wide // slots, ess_rows, 0)

    if kicks == n_wide:
        shared = bodies
    else:
        shared = ess_start
        kicked = []
        for t in every:

            def one_block(k, acc):
                listed = star_leaf[t * leaves // tiles, k]
                start = bodies + listed * stars
                return loop(
                    stars // ROWS, lambda g, part: on_bodies(start + g * ROWS, (t,), part), acc
                )

            kicked.append(lax.fori_loop(0, kicks, one_block, (total[t],))[0])
        total = tuple(kicked)
    total = loop(
        (ess_start + n_wide * GROUPS - shared) // ROWS,
        lambda g, acc: on_bodies(shared + g * ROWS, every, acc),
        total,
        BODY_UNROLL,
    )
    for t in every:
        for c in range(3):
            piece = jnp.sum(total[t][c], axis=0, keepdims=True)
            spot = (slice(c, c + 1), slice(t * LANES, (t + 1) * LANES))
            out[spot] = gal_vel[spot] + time_step * piece

    rest = states.at[pl.ds(0, n_narrow - 1)]
    pltpu.make_async_copy(rest, rest, pass_recv_sem).wait()

    def passed_rows(i, carry):
        n = lax.rem(narrow + 1 + i // halves, n_narrow)
        star_rows(n, lax.rem(i, halves))
        return carry

    loop((n_narrow - 1) * halves, passed_rows, 0, 12)
    pairs = n_narrow * halves

    pieces = []
    for t in range(0, stars, ROWS):
        mine = targets[t : t + ROWS, :]
        place = [column(mine, c) for c in range(3)]
        speed = [column(mine, 4 + c) for c in range(3)]

        def hermite(i, acc):
            rows = [spread(srow[i, c : c + 1, :]) for c in range(7)]
            dx, dy, dz = (rows[c] - place[c] for c in range(3))
            ux, uy, uz = (rows[4 + c] - speed[c] for c in range(3))
            inverse = lax.rsqrt(dx * dx + dy * dy + dz * dz + soften_sq)
            square = inverse * inverse
            weight = rows[3] * inverse * square
            approach = 3.0 * (dx * ux + dy * uy + dz * uz) * square
            return (
                acc[0] + dx * weight,
                acc[1] + dy * weight,
                acc[2] + dz * weight,
                acc[3] + (ux - dx * approach) * weight,
                acc[4] + (uy - dy * approach) * weight,
                acc[5] + (uz - dz * approach) * weight,
            )

        acc = loop(pairs, hermite, (zero,) * 6, STAR_UNROLL)

        def cell_pull(i, part):
            rows = [spread(crow[i, c : c + 1, :]) for c in range(4)]
            return pull(rows[:3], rows[3], place, part)

        acc = loop(n_wide // slots + 1, cell_pull, acc[:3]) + acc[3:]
        piece = jnp.zeros((ROWS, LANES), jnp.float32)
        for c in range(6):
            piece = jnp.where(lane8 == c, jnp.sum(acc[c], axis=1, keepdims=True), piece)
        pieces.append(piece)
    result = jnp.transpose(jnp.concatenate(pieces, axis=0))
    new_acc, new_jerk = result[0:3], result[3:6]
    vel_new = (
        svel + time_step * 0.5 * (sacc + new_acc) + step_sq / 12.0 * (sjerk - new_jerk)
    )
    vel_at = bodies + LANES
    out[:, vel_at : vel_at + stars] = vel_new
    out[:, bodies : bodies + stars] = (
        spos + time_step * 0.5 * (svel + vel_new) + step_sq / 12.0 * (sacc - new_acc)
    )

    pltpu.make_async_copy(some, some, send_sem).wait()
    pltpu.make_async_copy(few, few, cell_send_sem).wait()
    pltpu.make_async_copy(rest, rest, pass_send_sem).wait()


def unpack(packed, gal_out, pos_out, vel_out):
    bodies, stars = gal_out.shape[1], pos_out.shape[1]
    gal_out[...] = packed[:, 0:bodies]
    pos_out[...] = packed[:, bodies : bodies + stars]
    vel_out[...] = packed[:, bodies + LANES : bodies + LANES + stars]


def body(
    n_wide,
    n_narrow,
    star_pos,
    star_vel,
    star_mass,
    star_acc,
    star_jerk,
    gal_pos,
    gal_vel,
    gal_mass,
    group_of,
    let_send,
    star_leaf,
):
    n_dev = n_wide * n_narrow
    stars, bodies = star_pos.shape[1], gal_pos.shape[1]
    vmem = pl.BlockSpec(memory_space=pltpu.VMEM)
    f32 = jnp.float32
    i32 = jnp.int32
    hbm = pl.BlockSpec(memory_space=pltpu.HBM)
    packed = pl.pallas_call(
        functools.partial(kernel, n_wide, n_narrow),
        out_shape=jax.ShapeDtypeStruct((3, bodies + 2 * LANES), f32),
        in_specs=[hbm] * 11,
        out_specs=vmem,
        scratch_shapes=[
            pltpu.VMEM((3, stars), f32),
            pltpu.VMEM((3, stars), f32),
            pltpu.VMEM((1, stars), f32),
            pltpu.VMEM((3, stars), f32),
            pltpu.VMEM((3, stars), f32),
            pltpu.VMEM((3, bodies), f32),
            pltpu.VMEM((3, bodies), f32),
            pltpu.VMEM((1, bodies), f32),
            pltpu.VMEM((1, bodies), i32),
            pltpu.VMEM((1, n_wide), i32),
            pltpu.SMEM(star_leaf.shape, i32),
            pltpu.SemaphoreType.DMA((11,)),
            pltpu.VMEM((n_narrow, n_wide, 4, LANES), f32),
            pltpu.VMEM((n_wide, 1, LANES), f32),
            pltpu.VMEM((n_wide, 1, LANES), f32),
            pltpu.VMEM((bodies + n_wide * (stars + GROUPS), ROWS), f32),
            pltpu.VMEM((n_dev // 2, ROWS, LANES), f32),
            pltpu.VMEM((n_wide * GROUPS // LANES + 1, ROWS, LANES), f32),
            pltpu.SemaphoreType.DMA,
            pltpu.SemaphoreType.DMA,
            pltpu.SemaphoreType.DMA,
            pltpu.SemaphoreType.DMA,
            pltpu.SemaphoreType.DMA,
            pltpu.SemaphoreType.DMA,
        ],
        compiler_params=pltpu.CompilerParams(
            collective_id=0, has_side_effects=True, vmem_limit_bytes=24 << 20
        ),
    )(
        *(
            pltpu.with_memory_space_constraint(array, pltpu.HBM)
            for array in (
                star_pos,
                star_vel,
                star_mass.reshape(1, stars),
                star_acc,
                star_jerk,
                gal_pos,
                gal_vel,
                gal_mass.reshape(1, bodies),
                group_of.reshape(1, bodies),
                let_send.reshape(1, n_wide),
                star_leaf,
            )
        )
    )
    return pl.pallas_call(
        unpack,
        out_shape=(
            jax.ShapeDtypeStruct(gal_vel.shape, f32),
            jax.ShapeDtypeStruct(star_pos.shape, f32),
            jax.ShapeDtypeStruct(star_vel.shape, f32),
        ),
        in_specs=[vmem],
        out_specs=(vmem,) * 3,
        compiler_params=pltpu.CompilerParams(vmem_limit_bytes=1 << 20),
    )(packed)


def solution(mesh):
    both = ("wide", "narrow")
    columns, flat = P(None, both), P(both)
    return jax.shard_map(
        functools.partial(body, mesh.shape["wide"], mesh.shape["narrow"]),
        mesh=mesh,
        in_specs=(
            columns,
            columns,
            flat,
            columns,
            columns,
            columns,
            columns,
            flat,
            flat,
            P(both, None, None),
            P(both, None),
        ),
        out_specs=(columns, columns, columns),
        check_vma=False,
    )
```
